256 devices in a mesh: seq: 64 (over z, y, x_hi), head: 4 (over x_lo, core).
Axes of the slice: x: 4 (x_hi: 2, x_lo: 2; x = x_hi * 2 + x_lo), y: 4, z: 8, core: 2. Of those that a mesh axis runs over, the one named last changes fastest.
Arguments:
- query_rows: bfloat16 [2, 16384, 1024], P(None, 'seq', 'head'), may hold values from -70 to 70
- key_rows: bfloat16 [2, 16384, 1024], P(None, 'seq', 'head'), may hold values from -4.5 to 4.5
- value_rows: bfloat16 [2, 16384, 1024], P(None, 'seq', 'head'), may hold values from -6 to 6
- first_fast: float32 [4, 256, 512], P('head'), may hold values from -0.375 to 0.375
- third_fast: float32 [4, 256, 512], P('head'), may hold values from -0.375 to 0.375
- second_fast: float32 [4, 512, 256], P('head'), may hold values from -0.25 to 0.25
- out_proj: bfloat16 [1024, 1024], P('head'), may hold values from -0.1875 to 0.1875
- teacher: bfloat16 [2, 16384, 1024], P(None, 'seq'), may hold values from -31 to 31
Outputs:
- student: bfloat16 [2, 16384, 1024], P(None, 'seq', 'head')
- out_grad: float32 [1024, 1024], P('head')
- new_first: float32 [4, 256, 512], P('head')
- new_third: float32 [4, 256, 512], P('head')
- new_second: float32 [4, 512, 256], P('head')
- distill_loss: float32 [], replicated
The draws below stay inside these ranges and needn't reach their ends.
All inputs are finite; a program needn't handle non-finite values.
Results may differ from the reference program's by a relative error of at most 0.012.
Values may be sent and summed in bfloat16 or wider, within the bound.
A program may use at most 64 MiB of HBM per device.

```python
import math
import jax
import jax.numpy as jnp
from jax import lax

D = 1024
HEADS = 4
FF = 512
WINDOW = 256
NS_STEPS = 5
GROUPS = 2
HD = 256
GROUP = 16384


def draw_pairs(key):
    base_key = jax.random.fold_in(key, 711)
    key_part = jax.random.fold_in(base_key, 1)
    query_part = jax.random.fold_in(base_key, 2)
    total_rows = GROUPS * GROUP
    col_count = HEADS * HD
    keys_all = jnp.clip(jax.random.normal(key_part, (total_rows, col_count), jnp.float32), -4.5, 4.5)
    queries = jnp.clip(jax.random.normal(query_part, (total_rows, col_count), jnp.float32), -4.5, 4.5)
    return (queries.reshape(GROUPS, GROUP, col_count), keys_all.reshape(GROUPS, GROUP, col_count))


def draw_query_rows(key, part):
    return draw_pairs(key)[0].astype(jnp.bfloat16)


def draw_key_rows(key, part):
    return draw_pairs(key)[1].astype(jnp.bfloat16)


def draw_teacher(key, part):
    total_rows = GROUPS * GROUP
    noise = jnp.clip(jax.random.normal(jax.random.fold_in(key, 913), (total_rows, D), jnp.float32), -5.0, 5.0)
    ramp = 0.5 * jnp.exp(math.log(4.0) * jnp.arange(total_rows, dtype=jnp.float32) / (total_rows - 1))
    return (noise * ramp[:, None]).reshape(GROUPS, GROUP, D).astype(jnp.bfloat16)


def shard_levels(stream_key, extent, split, low, largest):
    def one(dim, parts):
        draws = jax.random.uniform(jax.random.fold_in(jax.random.fold_in(stream_key, 6), dim), (parts,), jnp.float32, low / len(split), largest / len(split))
        return jnp.repeat(jnp.exp(draws), extent[dim] // parts).reshape((-1,) + (1,) * (len(extent) - dim - 1))

    loudness = one(*split[0])
    for cut in split[1:]:
        loudness = loudness * one(*cut)
    return loudness


def centred(own_key, shape, spread, reach, split=(), kind=jnp.bfloat16):
    level = shard_levels(own_key, shape, split, -0.22, 0.18) if split else 1.0
    array = jax.random.normal(own_key, shape, jnp.float32) * spread * level
    return jnp.minimum(jnp.maximum(array, -reach), reach).astype(kind)


def setup_inputs(seed: int = 0) -> dict:
    streams_of = jax.random.split(jax.random.key(seed), 9)
    return {
        "query_rows": draw_query_rows(jax.random.fold_in(streams_of[8], 71), 0),
        "key_rows": draw_key_rows(jax.random.fold_in(streams_of[8], 71), 0),
        "value_rows": centred(streams_of[2], (GROUPS, GROUP, D), 1.0, 6.0, ((1, 64), (2, 4))),
        "first_fast": centred(streams_of[3], (HEADS, HD, FF), HD ** -0.5, 0.375, ((0, 4),), jnp.float32),
        "third_fast": centred(streams_of[4], (HEADS, HD, FF), HD ** -0.5, 0.375, ((0, 4),), jnp.float32),
        "second_fast": centred(streams_of[5], (HEADS, FF, HD), FF ** -0.5, 0.25, ((0, 4),), jnp.float32),
        "out_proj": centred(streams_of[6], (D, D), D ** -0.5, 0.1875, ((0, 4),)),
        "teacher": draw_teacher(jax.random.fold_in(streams_of[8], 71), 0),
    }


PRECISE = lax.Precision.HIGHEST
SCHULZ_COEFFS = (3.4445, -4.775, 2.0315)
LEARN_RATE = 0.5
EPSILON = 1e-06

def orthogonalize(matrix):
    current = matrix / (jnp.sqrt(jnp.sum(matrix * matrix)) + EPSILON)
    for sweep in range(NS_STEPS):
        gram_mat = jnp.dot(current, current.T, precision=PRECISE)
        poly_mat = SCHULZ_COEFFS[1] * gram_mat + SCHULZ_COEFFS[2] * jnp.dot(gram_mat, gram_mat, precision=PRECISE)
        current = SCHULZ_COEFFS[0] * current + jnp.dot(poly_mat, current, precision=PRECISE)
    return current

def fast_forward(w_one, w_three, w_two, inputs):
    gate_act = jnp.dot(inputs, w_one, precision=PRECISE)
    up_act = jnp.dot(inputs, w_three, precision=PRECISE)
    hidden = jax.nn.silu(gate_act) * up_act
    return (jnp.dot(hidden, w_two, precision=PRECISE), gate_act, up_act, hidden)

def fast_gradients(w_one, w_three, w_two, inputs, targets):
    unused, gate_act, up_act, hidden = fast_forward(w_one, w_three, w_two, inputs)
    grad_two = -jnp.dot(hidden.T, targets, precision=PRECISE)
    d_hidden = -jnp.dot(targets, w_two.T, precision=PRECISE)
    sigmoid_gate = jax.nn.sigmoid(gate_act)
    d_gate = d_hidden * up_act * sigmoid_gate * (1.0 + gate_act * (1.0 - sigmoid_gate))
    d_up = d_hidden * gate_act * sigmoid_gate
    grad_one = jnp.dot(inputs.T, d_gate, precision=PRECISE)
    grad_three = jnp.dot(inputs.T, d_up, precision=PRECISE)
    return (grad_one, grad_three, grad_two)

def fast_update(w_one, w_three, w_two, grads):
    return (w_one - LEARN_RATE * orthogonalize(grads[0]), w_three - LEARN_RATE * orthogonalize(grads[1]), w_two - LEARN_RATE * orthogonalize(grads[2].T).T)

def rms_scale(values):
    return values * lax.rsqrt(lax.optimization_barrier(jnp.mean(values * values, axis=-1, keepdims=True)) + EPSILON)

def window_attention(queries, keys, values):
    total_rows = queries.shape[0]
    blocks = total_rows // WINDOW
    pad_keys = jnp.concatenate([jnp.zeros((WINDOW, HD), keys.dtype), keys], axis=0)
    pad_values = jnp.concatenate([jnp.zeros((WINDOW, HD), values.dtype), values], axis=0)

    def one_block(block_idx):
        first_row = (block_idx * WINDOW).astype(jnp.int32)
        query_blk = lax.dynamic_slice_in_dim(queries, first_row, WINDOW, 0)
        key_blk = lax.dynamic_slice_in_dim(pad_keys, first_row, 2 * WINDOW, 0)
        value_blk = lax.dynamic_slice_in_dim(pad_values, first_row, 2 * WINDOW, 0)
        query_pos = first_row + jnp.arange(WINDOW, dtype=jnp.int32)
        key_pos = first_row - WINDOW + jnp.arange(2 * WINDOW, dtype=jnp.int32)
        scores = jnp.dot(query_blk, key_blk.T, preferred_element_type=jnp.float32) * (1.0 / math.sqrt(HD))
        spacing = query_pos[:, None] - key_pos[None, :]
        allowed = (spacing >= 0) & (spacing < WINDOW) & (key_pos[None, :] >= 0)
        masked = jnp.where(allowed, scores, -1e+30)
        top_score = lax.optimization_barrier(jnp.max(masked, axis=1, keepdims=True))
        expd = jnp.where(allowed, jnp.exp(masked - top_score), 0.0)
        weights = (expd / lax.optimization_barrier(jnp.sum(expd, axis=1, keepdims=True))).astype(jnp.bfloat16)
        return jnp.dot(weights, value_blk, preferred_element_type=jnp.float32)
    return lax.map(one_block, jnp.arange(blocks, dtype=jnp.int32)).reshape(total_rows, HD)

def reference(query_rows, key_rows, value_rows, first_fast, third_fast, second_fast, out_proj, teacher):
    total_rows = GROUPS * GROUP
    flat_q = query_rows.reshape(total_rows, D)
    flat_k = key_rows.reshape(total_rows, D)
    flat_v = value_rows.reshape(total_rows, D)
    mixed_heads = []
    firsts, thirds, seconds = ([], [], [])
    for head_idx in range(HEADS):
        lo_col = head_idx * HD
        hi_col = lo_col + HD
        attention = window_attention(flat_q[:, lo_col:hi_col], flat_k[:, lo_col:hi_col], flat_v[:, lo_col:hi_col]).reshape(GROUPS, GROUP, HD)
        w_one, w_three, w_two = (first_fast[head_idx], third_fast[head_idx], second_fast[head_idx])
        pieces = []
        for block_idx in range(GROUPS):
            q_float = query_rows[block_idx, :, lo_col:hi_col].astype(jnp.float32)
            k_float = key_rows[block_idx, :, lo_col:hi_col].astype(jnp.float32)
            v_float = value_rows[block_idx, :, lo_col:hi_col].astype(jnp.float32)
            fast_out = fast_forward(w_one, w_three, w_two, q_float)[0]
            pieces.append((attention[block_idx] + rms_scale(fast_out)).astype(jnp.bfloat16))
            grads = fast_gradients(w_one, w_three, w_two, k_float, v_float)
            w_one, w_three, w_two = fast_update(w_one, w_three, w_two, grads)
        mixed_heads.append(jnp.stack(pieces))
        firsts.append(w_one)
        thirds.append(w_three)
        seconds.append(w_two)
    mixed = jnp.concatenate(mixed_heads, axis=2).reshape(total_rows, D)
    summed = jnp.dot(mixed, out_proj, preferred_element_type=jnp.float32)
    student = summed.astype(jnp.bfloat16).reshape(GROUPS, GROUP, D)
    diff = summed - teacher.reshape(total_rows, D).astype(jnp.float32)
    resid = diff.astype(jnp.bfloat16)
    out_grad = jnp.dot(mixed.T, resid, preferred_element_type=jnp.float32) / math.sqrt(total_rows)
    distill_loss = jnp.sum(diff * diff) / (total_rows * D)
    return (student, out_grad, jnp.stack(firsts), jnp.stack(thirds), jnp.stack(seconds), distill_loss)
```

```python
import math

import jax
import jax.numpy as jnp
from jax import lax
from jax.experimental import pallas as pl
from jax.experimental.pallas import tpu as pltpu
from jax.sharding import PartitionSpec as P

F32 = jnp.float32
BF16 = jnp.bfloat16
C1, C3, C5 = (3.4445, -4.775, 2.0315)
LEARN_RATE = 0.5
EPSILON = 1e-06
NY, NX = 4, 2


def dot(a, b):
    return lax.dot_general(a, b, (((1,), (0,)), ((), ())), preferred_element_type=F32)


def dot_nt(a, b):
    return lax.dot_general(a, b, (((1,), (1,)), ((), ())), preferred_element_type=F32)


def dot_tn(a, b):
    return lax.dot_general(a, b, (((0,), (0,)), ((), ())), preferred_element_type=F32)


class Link:
    def __init__(self, send, recv):
        self.send, self.recv, self.used, self.open = send, recv, 0, []

    def take(self, count):
        first = self.used
        self.used += count
        return first

    def copy(self, src, dst, index, device):
        made = pltpu.make_async_remote_copy(
            src_ref=src, dst_ref=dst, send_sem=self.send.at[index], recv_sem=self.recv.at[index],
            device_id=device, device_id_type=pl.DeviceIdType.MESH)
        made.start()
        self.open.append(made)

    def arrive(self, dst, index, device):
        pltpu.make_async_remote_copy(
            src_ref=dst, dst_ref=dst, send_sem=self.send.at[index], recv_sem=self.recv.at[index],
            device_id=device, device_id_type=pl.DeviceIdType.MESH).wait_recv()

    def drain(self):
        for made in self.open:
            made.wait_send()


def by_distance(count):
    return sorted(range(1, count), key=lambda d: min(d, count - d))


def make_body(nz, ny, nx, nh, tok, hd, ff):
    fs, rp = ff // ny, hd // nz
    orow = hd // ny // (nz // 2)
    nseq = nz * ny * nx

    def body(q_ref, k_ref, v_ref, w1_ref, w3_ref, w2_ref, p_ref, t_ref,
             st_ref, og_ref, n1_ref, n3_ref, n2_ref, ls_ref,
             hk, hv, kg, vg, pc, tch, wb, acc, gs, rz, xs, xr, ga, xf, xh, xl, att, mx, rsd,
             ogs, oy, ozs, oz, oxs, oxr, oh, oa, ly, lz, lx, lh, send, recv, tsem):
        s = lax.axis_index("seq")
        h = lax.axis_index("head")
        x = lax.rem(s, nx)
        y = lax.rem(s // nx, ny)
        z = s // (nx * ny)
        news = (n1_ref, n3_ref, n2_ref)
        link = Link(send, recv)

        def at_z(zz):
            return ((zz * ny + y) * nx + x, h)

        def at_y(yy):
            return ((z * ny + yy) * nx + x, h)

        def hop(i, d, n):
            return lax.rem(i + d, n)

        def back(i, d, n):
            return lax.rem(i + n - d, n)

        at_x = ((z * ny + y) * nx + (1 - x), h)
        after = (lax.rem(s + 1, nseq), h)
        before = (lax.rem(s + nseq - 1, nseq), h)

        barrier = pltpu.get_barrier_semaphore()
        partners = [at_z(hop(z, d, nz)) for d in range(1, nz)]
        partners += [at_y(hop(y, d, ny)) for d in range(1, ny)]
        partners += [(s, hop(h, d, nh)) for d in range(1, nh)]
        partners += [at_x, after, before]
        for device in partners:
            pl.semaphore_signal(barrier, inc=1, device_id=device, device_id_type=pl.DeviceIdType.MESH)
        pl.semaphore_wait(barrier, len(partners))

        gat = [link.take(2 * (ny - 1)) for c in range(2)]

        def gather_send(c):
            for d in range(1, ny):
                device = at_y(hop(y, d, ny))
                link.copy(k_ref.at[c], kg.at[c, y], gat[c] + 2 * d - 2, device)
                link.copy(v_ref.at[c], vg.at[c, y], gat[c] + 2 * d - 1, device)
            kg[c, y] = k_ref[c]
            vg[c, y] = v_ref[c]

        def gather_wait(c):
            for d in range(1, ny):
                yy = back(y, d, ny)
                link.arrive(kg.at[c, yy], gat[c] + 2 * d - 2, at_y(yy))
                link.arrive(vg.at[c, yy], gat[c] + 2 * d - 1, at_y(yy))

        last = (s + 1) // nseq
        rim = link.take(4)

        def rim_send(c):
            slot = lax.rem(c + last, 2)
            link.copy(k_ref.at[c], hk.at[slot], rim + 2 * c, after)
            link.copy(v_ref.at[c], hv.at[slot], rim + 2 * c + 1, after)

        first = 1 - jnp.minimum(s, 1)

        def rim_wait(c):
            slot = lax.rem(c + first, 2)
            link.arrive(hk.at[slot], rim + 2 * c, before)
            link.arrive(hv.at[slot], rim + 2 * c + 1, before)

        prj = link.take(nh - 1)

        def columns(hh):
            return pl.ds(pl.multiple_of(hh * hd, hd), hd)

        def proj_send():
            for d in range(1, nh):
                hh = hop(h, d, nh)
                link.copy(p_ref.at[:, columns(hh)], pc.at[h], prj + d - 1, (s, hh))
            pc[h] = p_ref[:, columns(h)]

        def proj_wait():
            for d in range(1, nh):
                hh = back(h, d, nh)
                link.arrive(pc.at[hh], prj + d - 1, (s, hh))

        def grads(c):
            cols = pl.ds(pl.multiple_of(y * fs, fs), fs)
            w13 = jnp.concatenate([wb[0, :, cols], wb[1, :, cols]], axis=1)
            w2s = wb[2, :, cols]
            for yy in range(ny):
                kk, vv = kg[c, yy], vg[c, yy]
                gu = dot(kk, w13)
                g, u = gu[:, :fs], gu[:, fs:]
                dh = dot(vv, w2s)
                sg = jax.nn.sigmoid(g)
                act = g * sg
                dd = jnp.concatenate([dh * u * (sg + act * (1.0 - sg)), dh * act], axis=1).astype(BF16)
                hid = (act * u).astype(BF16)
                t13, t2 = dot_tn(kk, dd), dot_tn(vv, hid)
                if yy == 0:
                    acc[:, : 2 * fs] = t13
                    acc[:, 2 * fs:] = t2
                else:
                    acc[:, : 2 * fs] += t13
                    acc[:, 2 * fs:] += t2
            gs[c] = acc[...].astype(BF16).reshape(nz, rp, 3 * fs)

        rsz = [link.take(nz - 1) for c in range(2)]
        exx = [link.take(1) for c in range(2)]
        agz = [link.take(nz - 1) for c in range(2)]
        agy = [link.take((ny - 1) * nz) for c in range(2)]

        def rs_send(c):
            for d in range(1, nz):
                zz = hop(z, d, nz)
                link.copy(gs.at[c, zz], rz.at[c, d - 1], rsz[c] + d - 1, at_z(zz))

        def rs_finish(c):
            total = acc[pl.ds(pl.multiple_of(z * rp, rp), rp), :]
            for d in by_distance(nz):
                link.arrive(rz.at[c, d - 1], rsz[c] + d - 1, at_z(back(z, d, nz)))
                total = total + rz[c, d - 1].astype(F32)
            xs[c] = total.astype(BF16)
            link.copy(xs.at[c], xr.at[c], exx[c], at_x)

        def forward_y(c, zz, d):
            for e in range(1, ny):
                yy = hop(y, e, ny)
                link.copy(ga.at[c, y, zz], ga.at[c, y, zz], agy[c] + (e - 1) * nz + d, at_y(yy))

        def x_finish(c):
            link.arrive(xr.at[c], exx[c], at_x)
            ga[c, y, z] = (xs[c].astype(F32) + xr[c].astype(F32)).astype(BF16)
            for d in by_distance(nz):
                link.copy(ga.at[c, y, z], ga.at[c, y, z], agz[c] + d - 1, at_z(hop(z, d, nz)))
            forward_y(c, z, 0)

        def ag_forward(c):
            for d in by_distance(nz):
                zz = back(z, d, nz)
                link.arrive(ga.at[c, y, zz], agz[c] + d - 1, at_z(zz))
                forward_y(c, zz, d)

        def ag_wait(c):
            for e in range(1, ny):
                yy = back(y, e, ny)
                for d in range(nz):
                    zz = back(z, d, nz)
                    link.arrive(ga.at[c, yy, zz], agy[c] + (e - 1) * nz + d, at_y(yy))

        def put(m, value, low):
            xf[m] = value
            hi = value.astype(BF16)
            xh[m] = hi
            if low:
                xl[m] = (value - hi.astype(F32)).astype(BF16)

        def schulz(c):
            for m in range(3):
                full = jnp.concatenate(
                    [ga[c, yy].reshape(hd, 3 * fs)[:, m * fs:(m + 1) * fs] for yy in range(ny)], axis=1
                ).astype(F32)
                norm = jnp.sqrt(jnp.sum(full * full, keepdims=True)) + EPSILON
                put(m, full * (1.0 / norm), False)

            def coarse(step, carry):
                grams = [dot_nt(xh[m], xh[m]) for m in range(3)]
                for m in range(3):
                    small = grams[m].astype(BF16)
                    poly = C3 * grams[m] + C5 * dot(small, small)
                    put(m, C1 * xf[m] + dot(poly.astype(BF16), xh[m]), True)
                return carry

            def fine(step, carry):
                grams = [dot_nt(xh[m], xh[m]) for m in range(3)]
                for m in range(3):
                    gh = grams[m].astype(BF16)
                    gl = (grams[m] - gh.astype(F32)).astype(BF16)
                    square = dot(jnp.concatenate([gh, gl, gh], axis=1), jnp.concatenate([gh, gh, gl], axis=0))
                    poly = C3 * grams[m] + C5 * square
                    ph = poly.astype(BF16)
                    po = (poly - ph.astype(F32)).astype(BF16)
                    step_x = dot(jnp.concatenate([ph, po, ph], axis=1),
                                 jnp.concatenate([xh[m], xh[m], xl[m]], axis=0))
                    put(m, C1 * xf[m] + step_x, True)
                return carry

            lax.fori_loop(0, 2, coarse, 0)
            lax.fori_loop(0, 3, fine, 0)
            for m in range(3):
                news[m][...] += LEARN_RATE * xf[m]
                if c == 0:
                    wb[m] = news[m][...].astype(BF16)

        def attend(c):
            qq = q_ref[c]
            scale = 1.0 / math.sqrt(hd)
            row = lax.broadcasted_iota(jnp.int32, (tok, tok), 0)
            col = lax.broadcasted_iota(jnp.int32, (tok, tok), 1)
            own_ok = col <= row
            rim_ok = col > row + (first * tok if c == 0 else 0)
            own = jnp.where(own_ok, dot_nt(qq, k_ref[c]) * scale, -1e30)
            old = jnp.where(rim_ok, dot_nt(qq, hk[c]) * scale, -1e30)
            top = jnp.maximum(jnp.max(own, axis=1, keepdims=True), jnp.max(old, axis=1, keepdims=True))
            own = jnp.where(own_ok, jnp.exp(own - top), 0.0)
            old = jnp.where(rim_ok, jnp.exp(old - top), 0.0)
            inv = 1.0 / (jnp.sum(own, axis=1, keepdims=True) + jnp.sum(old, axis=1, keepdims=True))
            att[c] = dot((own * inv).astype(BF16), v_ref[c]) + dot((old * inv).astype(BF16), hv[c])

        def recall(c):
            qq = q_ref[c]
            g, u = dot(qq, wb[0]), dot(qq, wb[1])
            hid = (g * jax.nn.sigmoid(g) * u).astype(BF16)
            out = dot_nt(hid, wb[2])
            return out * lax.rsqrt(jnp.mean(out * out, axis=1, keepdims=True) + EPSILON)

        mxs = [link.take(nh - 1) for c in range(2)]

        def mix_send(c):
            for d in range(1, nh):
                link.copy(mx.at[c, h], mx.at[c, h], mxs[c] + d - 1, (s, hop(h, d, nh)))

        def mix_wait(c):
            for d in range(1, nh):
                hh = back(h, d, nh)
                link.arrive(mx.at[c, hh], mxs[c] + d - 1, (s, hh))

        def project(c):
            total = dot(mx[c, 0], pc[0])
            for hh in range(1, nh):
                total = total + dot(mx[c, hh], pc[hh])
            st_ref[c] = total.astype(BF16)
            diff = total - tch[c].astype(F32)
            rsd[c] = diff.astype(BF16)
            return jnp.sum((diff * diff).reshape(tok // 8, 8, hd // 128, 128), axis=(0, 2))

        teach = pltpu.make_async_copy(t_ref.at[:, :, columns(h)], tch, tsem)
        gather_send(0)
        teach.start()
        rim_send(0)
        rim_send(1)
        proj_send()
        gather_send(1)
        n1_ref[...] = w1_ref[...]
        n3_ref[...] = w3_ref[...]
        n2_ref[...] = w2_ref[...].T
        for m in range(3):
            wb[m] = news[m][...].astype(BF16)
        normed = recall(0)
        gather_wait(0)
        grads(0)
        rs_send(0)
        rim_wait(0)
        rim_wait(1)
        attend(0)
        mx[0, h] = (att[0] + normed).astype(BF16)
        mix_send(0)
        rs_finish(0)
        attend(1)
        x_finish(0)
        proj_wait()
        teach.wait()
        ag_forward(0)
        mix_wait(0)
        loss = project(0)
        ag_wait(0)
        schulz(0)
        gather_wait(1)
        grads(1)
        rs_send(1)
        mx[1, h] = (att[1] + recall(1)).astype(BF16)
        mix_send(1)
        rs_finish(1)
        mix_wait(1)
        loss = loss + project(1)

        osy = link.take(ny - 1)
        osz = link.take(nz - 1)
        osx = link.take(1)
        osh = link.take(nh - 1)
        oaz = link.take(nz - 1)
        oay = link.take((ny - 1) * nz)
        lsy, lsz, lsx, lsh = link.take(ny - 1), link.take(nz - 1), link.take(1), link.take(nh - 1)
        for hh in range(nh):
            part = (dot_tn(mx[0, hh], rsd[0]) + dot_tn(mx[1, hh], rsd[1])).astype(BF16)
            for yy in range(ny):
                for zz in range(nz):
                    top = yy * (hd // ny) + (zz // 2) * orow
                    left = (zz % 2) * (hd // 2)
                    ogs[yy, zz, hh] = part[top:top + orow, left:left + hd // 2]
        ly[y] = loss
        for d in range(1, ny):
            yy = hop(y, d, ny)
            link.copy(ogs.at[yy], oy.at[d - 1], osy + d - 1, at_y(yy))
            link.copy(ly.at[y], ly.at[y], lsy + d - 1, at_y(yy))
        x_finish(1)
        total = ogs[y].astype(F32)
        for d in range(1, ny):
            yy = back(y, d, ny)
            link.arrive(oy.at[d - 1], osy + d - 1, at_y(yy))
            link.arrive(ly.at[yy], lsy + d - 1, at_y(yy))
            total = total + oy[d - 1].astype(F32)
        ozs[...] = total.astype(BF16)
        lz[z] = jnp.sum(ly[...], axis=0)
        for d in by_distance(nz):
            zz = hop(z, d, nz)
            link.copy(ozs.at[zz], oz.at[d - 1], osz + d - 1, at_z(zz))
            link.copy(lz.at[z], lz.at[z], lsz + d - 1, at_z(zz))
        ag_forward(1)
        total = ozs[z].astype(F32)
        for d in by_distance(nz):
            zz = back(z, d, nz)
            link.arrive(oz.at[d - 1], osz + d - 1, at_z(zz))
            link.arrive(lz.at[zz], lsz + d - 1, at_z(zz))
            total = total + oz[d - 1].astype(F32)
        oxs[...] = total.astype(BF16)
        link.copy(oxs, oxr, osx, at_x)
        lx[x] = jnp.sum(lz[...], axis=0)
        link.copy(lx.at[x], lx.at[x], lsx, at_x)
        link.arrive(oxr, osx, at_x)
        link.arrive(lx.at[1 - x], lsx, at_x)
        oh[...] = (oxs[...].astype(F32) + oxr[...].astype(F32)).astype(BF16)
        lh[h] = jnp.sum(lx[...], axis=0)
        for d in range(1, nh):
            hh = hop(h, d, nh)
            link.copy(oh.at[hh], oa.at[y, z, h], osh + d - 1, (s, hh))
            link.copy(lh.at[h], lh.at[h], lsh + d - 1, (s, hh))
        oa[y, z, h] = oh[h]
        for d in range(1, nh):
            hh = back(h, d, nh)
            link.arrive(oa.at[y, z, hh], osh + d - 1, (s, hh))
            link.arrive(lh.at[hh], lsh + d - 1, (s, hh))

        def og_forward(zz, d):
            for e in range(1, ny):
                link.copy(oa.at[y, zz], oa.at[y, zz], oay + (e - 1) * nz + d, at_y(hop(y, e, ny)))

        for d in by_distance(nz):
            link.copy(oa.at[y, z], oa.at[y, z], oaz + d - 1, at_z(hop(z, d, nz)))
        og_forward(z, 0)
        ls_ref[...] = jnp.broadcast_to(jnp.sum(jnp.sum(lh[...], axis=0), keepdims=True), (8, 128))
        for d in by_distance(nz):
            zz = back(z, d, nz)
            link.arrive(oa.at[y, zz], oaz + d - 1, at_z(zz))
            og_forward(zz, d)
        ag_wait(1)
        schulz(1)
        for e in range(1, ny):
            yy = back(y, e, ny)
            for d in range(nz):
                link.arrive(oa.at[yy, back(z, d, nz)], oay + (e - 1) * nz + d, at_y(yy))
        for yy in range(ny):
            for zz in range(nz):
                top = yy * (hd // ny) + (zz // 2) * orow
                for hh in range(nh):
                    left = hh * hd + (zz % 2) * (hd // 2)
                    og_ref[top:top + orow, left:left + hd // 2] = oa[yy, zz, hh]
        link.drain()

    return body


def local(nh, query_rows, key_rows, value_rows, first_fast, third_fast, second_fast, out_proj, teacher):
    blocks, tok, hd = query_rows.shape
    ff = first_fast.shape[2]
    nseq = lax.axis_size("seq")
    nx, ny = NX, NY
    if nseq < 16:
        ny = 2
    nz = nseq // (nx * ny)
    width = teacher.shape[2]
    fs, rp = ff // ny, hd // nz
    orow = hd // ny // (nz // 2)
    vm = pltpu.VMEM
    piece = (nh, orow, hd // 2)
    sems = (2 * 2 * (ny - 1) + 4 + (nh - 1) + 2 * (2 * (nz - 1) + 1 + (ny - 1) * nz) + 2 * (nh - 1)
            + 2 * (ny - 1 + nz - 1 + 1 + nh - 1) + (nz - 1) + (ny - 1) * nz)
    spec = pl.BlockSpec(memory_space=pltpu.VMEM)
    student, grad, n1, n3, n2, loss = pl.pallas_call(
        make_body(nz, ny, nx, nh, tok, hd, ff),
        out_shape=(
            jax.ShapeDtypeStruct((2, tok, hd), BF16),
            jax.ShapeDtypeStruct((hd, width), BF16),
            jax.ShapeDtypeStruct((hd, ff), F32),
            jax.ShapeDtypeStruct((hd, ff), F32),
            jax.ShapeDtypeStruct((hd, ff), F32),
            jax.ShapeDtypeStruct((8, 128), F32),
        ),
        in_specs=[spec] * 7 + [pl.BlockSpec(memory_space=pl.ANY)],
        out_specs=(spec,) * 6,
        scratch_shapes=[
            vm((2, tok, hd), BF16), vm((2, tok, hd), BF16),
            vm((2, ny, tok, hd), BF16), vm((2, ny, tok, hd), BF16),
            vm((nh, hd, hd), BF16), vm((2, tok, hd), BF16),
            vm((3, hd, ff), BF16), vm((hd, 3 * fs), F32),
            vm((2, nz, rp, 3 * fs), BF16), vm((2, nz - 1, rp, 3 * fs), BF16),
            vm((2, rp, 3 * fs), BF16), vm((2, rp, 3 * fs), BF16),
            vm((2, ny, nz, rp, 3 * fs), BF16),
            vm((3, hd, ff), F32), vm((3, hd, ff), BF16), vm((3, hd, ff), BF16),
            vm((2, tok, hd), F32), vm((2, nh, tok, hd), BF16), vm((2, tok, hd), BF16),
            vm((ny, nz) + piece, BF16), vm((ny - 1, nz) + piece, BF16),
            vm((nz,) + piece, BF16), vm((nz - 1,) + piece, BF16),
            vm(piece, BF16), vm(piece, BF16), vm(piece, BF16),
            vm((ny, nz) + piece, BF16),
            vm((ny, 8, 128), F32), vm((nz, 8, 128), F32), vm((nx, 8, 128), F32), vm((nh, 8, 128), F32),
            pltpu.SemaphoreType.DMA((sems,)), pltpu.SemaphoreType.DMA((sems,)), pltpu.SemaphoreType.DMA,
        ],
        compiler_params=pltpu.CompilerParams(collective_id=0, has_side_effects=True, vmem_limit_bytes=56 << 20),
        name="student_step",
    )(query_rows, key_rows, value_rows, first_fast[0], third_fast[0], second_fast[0], out_proj, teacher)
    rows = blocks * tok * nseq
    out_grad = grad.astype(F32) / math.sqrt(rows)
    distill_loss = loss[0, 0] / (rows * width)
    return (student, out_grad, n1[None], n3[None], n2.T[None], distill_loss)


def solution(mesh):
    nh = mesh.shape["head"]

    def step(*args):
        return local(nh, *args)

    in_specs = (
        P(None, "seq", "head"),
        P(None, "seq", "head"),
        P(None, "seq", "head"),
        P("head", None, None),
        P("head", None, None),
        P("head", None, None),
        P("head", None),
        P(None, "seq", None),
    )
    out_specs = (
        P(None, "seq", "head"),
        P("head", None),
        P("head", None, None),
        P("head", None, None),
        P("head", None, None),
        P(),
    )
    return jax.shard_map(step, mesh=mesh, in_specs=in_specs, out_specs=out_specs, check_vma=False)
```

```python
import math

import jax
import jax.numpy as jnp
from jax import lax
from jax.experimental import pallas as pl
from jax.experimental.pallas import tpu as pltpu
from jax.sharding import PartitionSpec as P

F32 = jnp.float32
BF16 = jnp.bfloat16
C1, C3, C5 = (3.4445, -4.775, 2.0315)
LEARN_RATE = 0.5
EPSILON = 1e-06
NY, NX = 4, 2


def dot(a, b):
    return lax.dot_general(a, b, (((1,), (0,)), ((), ())), preferred_element_type=F32)


def dot_nt(a, b):
    return lax.dot_general(a, b, (((1,), (1,)), ((), ())), preferred_element_type=F32)


def dot_tn(a, b):
    return lax.dot_general(a, b, (((0,), (0,)), ((), ())), preferred_element_type=F32)


class Link:
    def __init__(self, send, recv):
        self.send, self.recv, self.used, self.open = send, recv, 0, []

    def take(self, count):
        first = self.used
        self.used += count
        return first

    def copy(self, src, dst, index, device):
        made = pltpu.make_async_remote_copy(
            src_ref=src, dst_ref=dst, send_sem=self.send.at[index], recv_sem=self.recv.at[index],
            device_id=device, device_id_type=pl.DeviceIdType.MESH)
        made.start()
        self.open.append(made)

    def arrive(self, dst, index, device):
        pltpu.make_async_remote_copy(
            src_ref=dst, dst_ref=dst, send_sem=self.send.at[index], recv_sem=self.recv.at[index],
            device_id=device, device_id_type=pl.DeviceIdType.MESH).wait_recv()

    def drain(self):
        for made in self.open:
            made.wait_send()


def by_distance(count):
    return sorted(range(1, count), key=lambda d: min(d, count - d))


def make_body(nz, ny, nx, nh, tok, hd, ff):
    fs, rp = ff // ny, hd // nz
    orow = hd // ny // (nz // 2)
    nseq = nz * ny * nx

    def body(q_ref, k_ref, v_ref, w1_ref, w3_ref, w2_ref, p_ref, t_ref,
             st_ref, oa, n1_ref, n3_ref, n2_ref, ls_ref,
             hk, hv, kg, vg, qv, w2v, pc, tch, wb, acc, gs, rz, xs, xr, ga, xf, xh, xl, att, mx, rsd,
             ogs, oy, ozs, oz, oxs, ox, ly, lz, lx, send, recv, tsem):
        s = lax.axis_index("seq")
        h = lax.axis_index("head")
        x = lax.rem(s, nx)
        y = lax.rem(s // nx, ny)
        z = s // (nx * ny)
        news = (n1_ref, n3_ref, n2_ref)
        link = Link(send, recv)

        def at_z(zz):
            return ((zz * ny + y) * nx + x, h)

        def at_y(yy):
            return ((z * ny + yy) * nx + x, h)

        def hop(i, d, n):
            return lax.rem(i + d, n)

        def back(i, d, n):
            return lax.rem(i + n - d, n)

        at_x = ((z * ny + y) * nx + (1 - x), h)

        def columns(hh):
            return pl.ds(pl.multiple_of(hh * hd, hd), hd)

        loads = []
        for i, (src, dst) in enumerate((
                (k_ref, kg.at[:, y]), (v_ref, vg.at[:, y]), (w1_ref, n1_ref), (w3_ref, n3_ref), (w2_ref, w2v),
                (q_ref, qv), (p_ref.at[:, columns(h)], pc.at[h]), (t_ref.at[:, :, columns(h)], tch))):
            loads.append(pltpu.make_async_copy(src, dst, tsem.at[i]))
            loads[-1].start()
        barrier = pltpu.get_barrier_semaphore()
        partners = [at_z(hop(z, d, nz)) for d in range(1, nz)]
        partners += [at_y(hop(y, d, ny)) for d in range(1, ny)]
        partners += [(s, hop(h, d, nh)) for d in range(1, nh)]
        partners += [((zz * ny + y) * nx + 1 - x, h) for zz in (z, hop(z, 1, nz), back(z, 1, nz))]
        partners += [(at_x[0], hop(h, d, nh)) for d in range(1, nh)]
        for device in partners:
            pl.semaphore_signal(barrier, inc=1, device_id=device, device_id_type=pl.DeviceIdType.MESH)
        pl.semaphore_wait(barrier, len(partners))

        gat = [link.take(2 * (ny - 1)) for c in range(2)]

        def gather_send(c):
            for d in by_distance(ny):
                if c == 0 and d == 2:
                    continue
                device = at_y(hop(y, d, ny))
                pair = ((k_ref, kg, 2), (v_ref, vg, 1))
                for src, dst, i in pair if d == 1 else pair[::-1]:
                    link.copy(src.at[c], dst.at[c, y], gat[c] + 2 * d - i, device)

        def gather_pass():
            if ny == 4:
                for d, ref, i in ((1, kg, 2), (3, vg, 1)):
                    yy = back(y, d, ny)
                    link.arrive(ref.at[0, yy], gat[0] + 2 * d - i, at_y(yy))
                    link.copy(ref.at[0, yy], ref.at[0, yy], gat[0] + 4 - i, at_y(hop(y, d, ny)))

        def gather_wait(c, d):
            yy = back(y, d, ny)
            passed = c == 0 and ny == 4
            if not (passed and d == 1):
                link.arrive(kg.at[c, yy], gat[c] + 2 * d - 2, at_y(yy))
            if not (passed and d == 3):
                link.arrive(vg.at[c, yy], gat[c] + 2 * d - 1, at_y(yy))

        first = 1 - jnp.minimum(s, 1)
        rim = link.take(4)
        held = back(y, x, ny)
        ahead = lax.rem(z + x * (1 - jnp.minimum(y, 1)), nz)
        behind = back(z, (1 - x) * (1 - jnp.minimum(y, 1)), nz)

        def rim_send(c):
            device = ((ahead * ny + y) * nx + 1 - x, h)
            link.copy(kg.at[c, held], hk.at[c], rim + 2 * c, device)
            link.copy(vg.at[c, held], hv.at[c], rim + 2 * c + 1, device)

        def rim_wait(c):
            device = ((behind * ny + y) * nx + 1 - x, h)
            link.arrive(hk.at[c], rim + 2 * c, device)
            link.arrive(hv.at[c], rim + 2 * c + 1, device)

        prj = link.take(nh - 1)

        def proj_send():
            for d in range(1, nh):
                hh = hop(h, d, nh)
                link.copy(p_ref.at[:, columns(hh)], pc.at[h], prj + d - 1, (s, hh))

        def proj_wait():
            for d in range(1, nh):
                hh = back(h, d, nh)
                link.arrive(pc.at[hh], prj + d - 1, (s, hh))

        def grads(c):
            cols = pl.ds(pl.multiple_of(y * fs, fs), fs)
            w13 = jnp.concatenate([wb[0, :, cols], wb[1, :, cols]], axis=1)
            w2s = wb[2, :, cols]
            for d in [0] + by_distance(ny):
                if d and c == 0:
                    gather_wait(c, d)
                yy = back(y, d, ny)
                kk, vv = kg[c, yy], vg[c, yy]
                gu = dot(kk, w13)
                g, u = gu[:, :fs], gu[:, fs:]
                dh = dot(vv, w2s)
                sg = jax.nn.sigmoid(g)
                act = g * sg
                dd = jnp.concatenate([dh * u * (sg + act * (1.0 - sg)), dh * act], axis=1).astype(BF16)
                hid = (act * u).astype(BF16)
                t13, t2 = dot_tn(kk, dd), dot_tn(vv, hid)
                if d == 0:
                    acc[:, : 2 * fs] = t13
                    acc[:, 2 * fs:] = t2
                else:
                    acc[:, : 2 * fs] += t13
                    acc[:, 2 * fs:] += t2
            gs[c] = acc[...].astype(BF16).reshape(nz, rp, 3 * fs)

        rsz = [link.take(nz - 1) for c in range(2)]
        exx = [link.take(1) for c in range(2)]
        agz = [link.take(nz - 1) for c in range(2)]
        agy = [link.take((ny - 1) * nz) for c in range(2)]

        def rs_send(c):
            for d in range(1, nz):
                zz = hop(z, d, nz)
                link.copy(gs.at[c, zz], rz.at[c, d - 1], rsz[c] + d - 1, at_z(zz))

        def rs_finish(c):
            total = acc[pl.ds(pl.multiple_of(z * rp, rp), rp), :]
            for d in by_distance(nz):
                link.arrive(rz.at[c, d - 1], rsz[c] + d - 1, at_z(back(z, d, nz)))
                total = total + rz[c, d - 1].astype(F32)
            xs[c] = total.astype(BF16)
            link.copy(xs.at[c], xr.at[c], exx[c], at_x)

        def forward_y(c, zz, d):
            for e in range(1, ny):
                yy = hop(y, e, ny)
                link.copy(ga.at[c, y, zz], ga.at[c, y, zz], agy[c] + (e - 1) * nz + d, at_y(yy))

        def x_finish(c):
            link.arrive(xr.at[c], exx[c], at_x)
            ga[c, y, z] = (xs[c].astype(F32) + xr[c].astype(F32)).astype(BF16)
            for d in by_distance(nz):
                link.copy(ga.at[c, y, z], ga.at[c, y, z], agz[c] + d - 1, at_z(hop(z, d, nz)))
            forward_y(c, z, 0)

        def ag_forward(c):
            for d in by_distance(nz):
                zz = back(z, d, nz)
                link.arrive(ga.at[c, y, zz], agz[c] + d - 1, at_z(zz))
                forward_y(c, zz, d)

        def ag_wait(c):
            for e in range(1, ny):
                yy = back(y, e, ny)
                for d in range(nz):
                    zz = back(z, d, nz)
                    link.arrive(ga.at[c, yy, zz], agy[c] + (e - 1) * nz + d, at_y(yy))

        def put(m, value, low):
            xf[m] = value
            hi = value.astype(BF16)
            xh[m] = hi
            if low:
                xl[m] = (value - hi.astype(F32)).astype(BF16)

        def schulz_start(c):
            for m in range(3):
                full = jnp.concatenate(
                    [ga[c, yy].reshape(hd, 3 * fs)[:, m * fs:(m + 1) * fs] for yy in range(ny)], axis=1
                ).astype(F32)
                norm = jnp.sqrt(jnp.sum(full * full, keepdims=True)) + EPSILON
                put(m, full * (1.0 / norm), False)

        def coarse(step, carry):
            grams = [dot_nt(xh[m], xh[m]) for m in range(3)]
            small = [gram.astype(BF16) for gram in grams]
            polys = [(C3 * grams[m] + C5 * dot(small[m], small[m])).astype(BF16) for m in range(3)]
            for m in range(3):
                put(m, C1 * xf[m] + dot(polys[m], xh[m]), True)
            return carry

        def fine(step, carry):
            grams = [dot_nt(xh[m], xh[m]) for m in range(3)]
            polys = []
            for m in range(3):
                gh = grams[m].astype(BF16)
                gl = (grams[m] - gh.astype(F32)).astype(BF16)
                square = dot(jnp.concatenate([gh, gl, gh], axis=1), jnp.concatenate([gh, gh, gl], axis=0))
                polys.append(C3 * grams[m] + C5 * square)
            for m in range(3):
                ph = polys[m].astype(BF16)
                po = (polys[m] - ph.astype(F32)).astype(BF16)
                step_x = dot(jnp.concatenate([ph, po, ph], axis=1),
                             jnp.concatenate([xh[m], xh[m], xl[m]], axis=0))
                put(m, C1 * xf[m] + step_x, True)
            return carry

        def schulz_coarse():
            lax.fori_loop(0, 2, coarse, 0)

        def schulz_fine(count):
            lax.fori_loop(0, count, fine, 0)

        def schulz_end(c):
            for m in range(3):
                news[m][...] += LEARN_RATE * xf[m]
                if c == 0:
                    wb[m] = news[m][...].astype(BF16)

        def attend(c):
            qq = qv[c]
            slot = c if c == 0 else 1 - first
            scale = 1.0 / math.sqrt(hd)
            row = lax.broadcasted_iota(jnp.int32, (tok, tok), 0)
            col = lax.broadcasted_iota(jnp.int32, (tok, tok), 1)
            own_ok = col <= row
            rim_ok = col > row + (first * tok if c == 0 else 0)
            own = jnp.where(own_ok, dot_nt(qq, kg[c, y]) * scale, -1e30)
            old = jnp.where(rim_ok, dot_nt(qq, hk[slot]) * scale, -1e30)
            top = jnp.maximum(jnp.max(own, axis=1, keepdims=True), jnp.max(old, axis=1, keepdims=True))
            own = jnp.where(own_ok, jnp.exp(own - top), 0.0)
            old = jnp.where(rim_ok, jnp.exp(old - top), 0.0)
            inv = 1.0 / (jnp.sum(own, axis=1, keepdims=True) + jnp.sum(old, axis=1, keepdims=True))
            return dot((own * inv).astype(BF16), vg[c, y]) + dot((old * inv).astype(BF16), hv[slot])

        def recall(c):
            qq = qv[c]
            g, u = dot(qq, wb[0]), dot(qq, wb[1])
            hid = (g * jax.nn.sigmoid(g) * u).astype(BF16)
            out = dot_nt(hid, wb[2])
            return out * lax.rsqrt(jnp.mean(out * out, axis=1, keepdims=True) + EPSILON)

        mxs = [link.take(nh - 1) for c in range(2)]

        twin = h + 1 - 2 * lax.rem(h, 2)
        near = lax.rem(h + 2, nh)
        far = lax.rem(twin + 2, nh)

        def mix_send(c):
            if nh == 4:
                link.copy(mx.at[c, h], mx.at[c, h], mxs[c], (s, near))
            link.copy(mx.at[c, h], mx.at[c, h], mxs[c] + nh - 2, (s, twin))

        def mix_pass(c):
            if nh == 4:
                link.arrive(mx.at[c, near], mxs[c], (s, near))
                link.copy(mx.at[c, near], mx.at[c, near], mxs[c] + 1, (s, twin))

        def mix_wait(c):
            link.arrive(mx.at[c, twin], mxs[c] + nh - 2, (s, twin))
            if nh == 4:
                link.arrive(mx.at[c, far], mxs[c] + 1, (s, twin))

        def project(c):
            total = dot(mx[c, 0], pc[0])
            for hh in range(1, nh):
                total = total + dot(mx[c, hh], pc[hh])
            st_ref[c] = total.astype(BF16)
            diff = total - tch[c].astype(F32)
            rsd[c] = diff.astype(BF16)
            return jnp.sum((diff * diff).reshape(tok // 8, 8, hd // 128, 128), axis=(0, 2))

        osy = link.take(ny - 1)
        osz = link.take(nz - 1)
        osx = link.take(nx * nh - 1)
        oaz = link.take(nz - 1)
        oay = link.take((ny - 1) * nz)
        lsy, lsz, lsx = link.take(ny - 1), link.take(nz - 1), link.take(nx * nh - 1)
        others = [(dx, dh) for dx in range(nx) for dh in range(nh)][1:]

        def at_xh(dx, dh, sign):
            hh = hop(h, dh, nh) if sign > 0 else back(h, dh, nh)
            xx = hop(x, dx, nx)
            return xx, hh, ((z * ny + y) * nx + xx, hh)

        def stage_grad(unused):
            for hh in range(nh):
                part = (dot_tn(mx[0, hh], rsd[0]) + dot_tn(mx[1, hh], rsd[1])).astype(BF16)
                for yy in range(ny):
                    for zz in range(nz):
                        top = yy * (hd // ny) + (zz // 2) * orow
                        left = (zz % 2) * (hd // 2)
                        ogs[yy, zz, hh] = part[top:top + orow, left:left + hd // 2]
            for d in by_distance(ny):
                yy = hop(y, d, ny)
                link.copy(ogs.at[yy], oy.at[d - 1], osy + d - 1, at_y(yy))
                link.copy(ly.at[y], ly.at[y], lsy + d - 1, at_y(yy))

        def stage_y(unused):
            total = ogs[y].astype(F32)
            for d in by_distance(ny):
                yy = back(y, d, ny)
                link.arrive(oy.at[d - 1], osy + d - 1, at_y(yy))
                link.arrive(ly.at[yy], lsy + d - 1, at_y(yy))
                total = total + oy[d - 1].astype(F32)
            ozs[...] = total.astype(BF16)
            lz[z] = jnp.sum(ly[...], axis=0)
            for d in by_distance(nz):
                zz = hop(z, d, nz)
                link.copy(ozs.at[zz], oz.at[d - 1], osz + d - 1, at_z(zz))
                link.copy(lz.at[z], lz.at[z], lsz + d - 1, at_z(zz))

        def stage_z(unused):
            total = ozs[z].astype(F32)
            for d in by_distance(nz):
                zz = back(z, d, nz)
                link.arrive(oz.at[d - 1], osz + d - 1, at_z(zz))
                link.arrive(lz.at[zz], lsz + d - 1, at_z(zz))
                total = total + oz[d - 1].astype(F32)
            oxs[...] = total.astype(BF16)
            lx[x, h] = jnp.sum(lz[...], axis=0)
            for i, (dx, dh) in enumerate(others):
                xx, hh, device = at_xh(dx, dh, 1)
                link.copy(oxs.at[hh], ox.at[x, h], osx + i, device)
                link.copy(lx.at[x, h], lx.at[x, h], lsx + i, device)
            ox[x, h] = oxs[h]

        def og_forward(zz, d):
            for e in by_distance(ny):
                link.copy(oa.at[y, zz], oa.at[y, zz], oay + (e - 1) * nz + d, at_y(hop(y, e, ny)))

        def stage_x(unused):
            for i, (dx, dh) in enumerate(others):
                xx, hh, device = at_xh(dx, dh, -1)
                link.arrive(ox.at[xx, hh], osx + i, device)
                link.arrive(lx.at[xx, hh], lsx + i, device)
            oa[y, z] = sum(ox[i].astype(F32) for i in range(nx)).astype(BF16)
            for d in by_distance(nz):
                link.copy(oa.at[y, z], oa.at[y, z], oaz + d - 1, at_z(hop(z, d, nz)))
            og_forward(z, 0)
            ls_ref[...] = jnp.sum(lx[...], axis=(0, 1))

        def stage_all(unused):
            for d in by_distance(nz):
                zz = back(z, d, nz)
                link.arrive(oa.at[y, zz], oaz + d - 1, at_z(zz))
                og_forward(zz, d)

        def stage_wait(unused):
            for e in by_distance(ny):
                yy = back(y, e, ny)
                for d in range(nz):
                    link.arrive(oa.at[yy, back(z, d, nz)], oay + (e - 1) * nz + d, at_y(yy))

        gather_send(0)
        for move in loads[2:]:
            move.wait()
        n2_ref[...] = w2v[...].T
        for m in range(3):
            wb[m] = news[m][...].astype(BF16)
        gather_pass()
        att[0] = recall(0)
        for move in loads[:2]:
            move.wait()
        grads(0)
        rs_send(0)
        rim_send(0)
        gather_send(1)
        proj_send()
        rs_finish(0)
        rim_wait(0)
        mx[0, h] = (att[0] + attend(0)).astype(BF16)
        x_finish(0)
        mix_send(0)
        ag_forward(0)
        for d in by_distance(ny):
            gather_wait(1, d)
        rim_send(1)
        mix_pass(0)
        mix_wait(0)
        proj_wait()
        loss = project(0)
        ag_wait(0)
        schulz_start(0)
        schulz_coarse()
        schulz_fine(3)
        schulz_end(0)
        grads(1)
        rs_send(1)
        rim_wait(1)
        att[1] = attend(1)
        mx[1, h] = (att[1] + recall(1)).astype(BF16)
        mix_send(1)
        mix_pass(1)
        rs_finish(1)
        mix_wait(1)
        ly[y] = loss + project(1)
        stage_grad(0)
        x_finish(1)
        ag_forward(1)
        stage_y(0)
        ag_wait(1)
        schulz_start(1)
        schulz_coarse()
        stage_z(0)
        schulz_fine(1)
        stage_x(0)
        schulz_fine(2)
        schulz_end(1)
        stage_all(0)
        stage_wait(0)
        link.drain()

    return body


def make_finish(nz, ny, nh, hd, grad_scale, loss_scale):
    orow = hd // ny // (nz // 2)

    def finish(st, oa, a1, a3, a2, ls, st_ref, og_ref, n1_ref, n3_ref, n2_ref, ls_ref, og, w2, sem):
        moves = [pltpu.make_async_copy(src, dst, sem.at[i]) for i, (src, dst) in enumerate((
            (st, st_ref), (a1, n1_ref), (a3, n3_ref), (w2, n2_ref), (og, og_ref)))]
        for move in moves[:3]:
            move.start()
        w2[...] = a2[...].T
        moves[3].start()
        for yy in range(ny):
            for zz in range(nz):
                top = yy * (hd // ny) + (zz // 2) * orow
                for hh in range(nh):
                    left = hh * hd + (zz % 2) * (hd // 2)
                    og[top:top + orow, left:left + hd // 2] = oa[yy, zz, hh].astype(F32) * grad_scale
        moves[4].start()
        ls_ref[0, 0] = jnp.sum(ls[...]) * loss_scale
        for move in moves:
            move.wait()

    return finish


def local(nh, query_rows, key_rows, value_rows, first_fast, third_fast, second_fast, out_proj, teacher):
    blocks, tok, hd = query_rows.shape
    ff = first_fast.shape[2]
    nseq = lax.axis_size("seq")
    nx, ny = NX, NY
    if nseq < 16:
        ny = 2
    nz = nseq // (nx * ny)
    width = teacher.shape[2]
    fs, rp = ff // ny, hd // nz
    orow = hd // ny // (nz // 2)
    vm = pltpu.VMEM
    piece = (nh, orow, hd // 2)
    sems = (2 * 2 * (ny - 1) + 4 + (nh - 1) + 2 * (2 * (nz - 1) + 1 + (ny - 1) * nz) + 2 * (nh - 1)
            + 2 * (ny - 1 + nz - 1 + nx * nh - 1) + (nz - 1) + (ny - 1) * nz)
    spec = pl.BlockSpec(memory_space=pltpu.VMEM)
    parts = pl.pallas_call(
        make_body(nz, ny, nx, nh, tok, hd, ff),
        out_shape=(
            jax.ShapeDtypeStruct((2, tok, hd), BF16),
            jax.ShapeDtypeStruct((ny, nz) + piece, BF16),
            jax.ShapeDtypeStruct((hd, ff), F32),
            jax.ShapeDtypeStruct((hd, ff), F32),
            jax.ShapeDtypeStruct((hd, ff), F32),
            jax.ShapeDtypeStruct((8, 128), F32),
        ),
        in_specs=[pl.BlockSpec(memory_space=pl.ANY)] * 8,
        out_specs=(spec,) * 6,
        scratch_shapes=[
            vm((2, tok, hd), BF16), vm((2, tok, hd), BF16),
            vm((2, ny, tok, hd), BF16), vm((2, ny, tok, hd), BF16),
            vm((2, tok, hd), BF16), vm((ff, hd), F32),
            vm((nh, hd, hd), BF16), vm((2, tok, hd), BF16),
            vm((3, hd, ff), BF16), vm((hd, 3 * fs), F32),
            vm((2, nz, rp, 3 * fs), BF16), vm((2, nz - 1, rp, 3 * fs), BF16),
            vm((2, rp, 3 * fs), BF16), vm((2, rp, 3 * fs), BF16),
            vm((2, ny, nz, rp, 3 * fs), BF16),
            vm((3, hd, ff), F32), vm((3, hd, ff), BF16), vm((3, hd, ff), BF16),
            vm((2, tok, hd), F32), vm((2, nh, tok, hd), BF16), vm((2, tok, hd), BF16),
            vm((ny, nz) + piece, BF16), vm((ny - 1, nz) + piece, BF16),
            vm((nz,) + piece, BF16), vm((nz - 1,) + piece, BF16),
            vm(piece, BF16), vm((nx,) + piece, BF16),
            vm((ny, 8, 128), F32), vm((nz, 8, 128), F32), vm((nx, nh, 8, 128), F32),
            pltpu.SemaphoreType.DMA((sems,)), pltpu.SemaphoreType.DMA((sems,)), pltpu.SemaphoreType.DMA((8,)),
        ],
        compiler_params=pltpu.CompilerParams(collective_id=0, has_side_effects=True, vmem_limit_bytes=56 << 20),
        name="student_step",
    )(query_rows, key_rows, value_rows, first_fast[0], third_fast[0], second_fast[0], out_proj, teacher)
    rows = blocks * tok * nseq
    hbm = pl.BlockSpec(memory_space=pl.ANY)
    student, out_grad, n1, n3, n2, loss = pl.pallas_call(
        make_finish(nz, ny, nh, hd, 1.0 / math.sqrt(rows), 1.0 / (rows * width)),
        out_shape=(
            jax.ShapeDtypeStruct((2, tok, hd), BF16),
            jax.ShapeDtypeStruct((hd, width), F32),
            jax.ShapeDtypeStruct((hd, ff), F32),
            jax.ShapeDtypeStruct((hd, ff), F32),
            jax.ShapeDtypeStruct((ff, hd), F32),
            jax.ShapeDtypeStruct((1, 1), F32),
        ),
        in_specs=[spec] * 6,
        out_specs=(hbm,) * 5 + (pl.BlockSpec(memory_space=pltpu.SMEM),),
        scratch_shapes=[vm((hd, width), F32), vm((ff, hd), F32), pltpu.SemaphoreType.DMA((5,))],
        name="finish",
    )(*parts)
    return (student, out_grad, n1[None], n3[None], n2[None], loss.reshape(()))


def solution(mesh):
    nh = mesh.shape["head"]

    def step(*args):
        return local(nh, *args)

    in_specs = (
        P(None, "seq", "head"),
        P(None, "seq", "head"),
        P(None, "seq", "head"),
        P("head", None, None),
        P("head", None, None),
        P("head", None, None),
        P("head", None),
        P(None, "seq", None),
    )
    out_specs = (
        P(None, "seq", "head"),
        P("head", None),
        P("head", None, None),
        P("head", None, None),
        P("head", None, None),
        P(),
    )
    return jax.shard_map(step, mesh=mesh, in_specs=in_specs, out_specs=out_specs, check_vma=False)
```

```python
import math

import jax
import jax.numpy as jnp
from jax import lax
from jax.experimental import pallas as pl
from jax.experimental.pallas import tpu as pltpu
from jax.sharding import PartitionSpec as P

F32 = jnp.float32
BF16 = jnp.bfloat16
C1, C3, C5 = (3.4445, -4.775, 2.0315)
LEARN_RATE = 0.5
EPSILON = 1e-06
NY, NX = 4, 2


def dot(a, b):
    return lax.dot_general(a, b, (((1,), (0,)), ((), ())), preferred_element_type=F32)


def dot_nt(a, b):
    return lax.dot_general(a, b, (((1,), (1,)), ((), ())), preferred_element_type=F32)


def dot_tn(a, b):
    return lax.dot_general(a, b, (((0,), (0,)), ((), ())), preferred_element_type=F32)


class Link:
    def __init__(self, send, recv):
        self.send, self.recv, self.used, self.open = send, recv, 0, []

    def take(self, count):
        first = self.used
        self.used += count
        return first

    def copy(self, src, dst, index, device):
        made = pltpu.make_async_remote_copy(
            src_ref=src, dst_ref=dst, send_sem=self.send.at[index], recv_sem=self.recv.at[index],
            device_id=device, device_id_type=pl.DeviceIdType.MESH)
        made.start()
        self.open.append(made)

    def arrive(self, dst, index, device):
        pltpu.make_async_remote_copy(
            src_ref=dst, dst_ref=dst, send_sem=self.send.at[index], recv_sem=self.recv.at[index],
            device_id=device, device_id_type=pl.DeviceIdType.MESH).wait_recv()

    def drain(self):
        for made in self.open:
            made.wait_send()


def by_distance(count):
    return sorted(range(1, count), key=lambda d: min(d, count - d))


def far_first(count):
    return by_distance(count)[::-1]


def make_body(nz, ny, nx, nh, tok, hd, ff):
    fs, rp = ff // ny, hd // nz
    orow = hd // ny // (nz // 2)
    nseq = nz * ny * nx

    def body(q_ref, k_ref, v_ref, w1_ref, w3_ref, w2_ref, p_ref, t_ref,
             st_ref, oa, n1_ref, n3_ref, n2_ref, ls_ref,
             hk, hv, kg, vg, qv, w2v, n2v, pc, tch, wb, acc, gs, rz, xs, xr, ga, xf, xh, xl, att, mx, rsd,
             ogs, oy, ozs, oz, oxs, ox, ly, lz, lx, send, recv, tsem):
        s = lax.axis_index("seq")
        h = lax.axis_index("head")
        x = lax.rem(s, nx)
        y = lax.rem(s // nx, ny)
        z = s // (nx * ny)
        news = (n1_ref, n3_ref, n2v)
        link = Link(send, recv)

        def at_z(zz):
            return ((zz * ny + y) * nx + x, h)

        def at_y(yy):
            return ((z * ny + yy) * nx + x, h)

        def hop(i, d, n):
            return lax.rem(i + d, n)

        def back(i, d, n):
            return lax.rem(i + n - d, n)

        at_x = ((z * ny + y) * nx + (1 - x), h)

        def columns(hh):
            return pl.ds(pl.multiple_of(hh * hd, hd), hd)

        loads = []
        for i, (src, dst) in enumerate((
                (k_ref, kg.at[:, y]), (v_ref, vg.at[:, y]), (w1_ref, n1_ref), (w3_ref, n3_ref), (w2_ref, w2v),
                (q_ref, qv), (p_ref.at[:, columns(h)], pc.at[h]), (t_ref.at[:, :, columns(h)], tch))):
            loads.append(pltpu.make_async_copy(src, dst, tsem.at[i]))
            loads[-1].start()
        barrier = pltpu.get_barrier_semaphore()
        partners = [at_z(hop(z, d, nz)) for d in range(1, nz)]
        partners += [at_y(hop(y, d, ny)) for d in range(1, ny)]
        partners += [(s, hop(h, d, nh)) for d in range(1, nh)]
        partners += [((zz * ny + y) * nx + 1 - x, h) for zz in (z, hop(z, 1, nz), back(z, 1, nz))]
        partners += [(at_x[0], hop(h, d, nh)) for d in range(1, nh)]
        for device in partners:
            pl.semaphore_signal(barrier, inc=1, device_id=device, device_id_type=pl.DeviceIdType.MESH)
        pl.semaphore_wait(barrier, len(partners))

        gat = [link.take(2 * (ny - 1)) for c in range(2)]

        def gather_send(c):
            for d in by_distance(ny):
                if c == 0 and d == 2:
                    continue
                device = at_y(hop(y, d, ny))
                pair = ((k_ref, kg, 2), (v_ref, vg, 1))
                for src, dst, i in pair if d == 1 else pair[::-1]:
                    link.copy(src.at[c], dst.at[c, y], gat[c] + 2 * d - i, device)

        def gather_pass():
            if ny == 4:
                for d, ref, i in ((1, kg, 2), (3, vg, 1)):
                    yy = back(y, d, ny)
                    link.arrive(ref.at[0, yy], gat[0] + 2 * d - i, at_y(yy))
                    link.copy(ref.at[0, yy], ref.at[0, yy], gat[0] + 4 - i, at_y(hop(y, d, ny)))

        def gather_wait(c, d):
            yy = back(y, d, ny)
            passed = c == 0 and ny == 4
            if not (passed and d == 1):
                link.arrive(kg.at[c, yy], gat[c] + 2 * d - 2, at_y(yy))
            if not (passed and d == 3):
                link.arrive(vg.at[c, yy], gat[c] + 2 * d - 1, at_y(yy))

        first = 1 - jnp.minimum(s, 1)
        rim = link.take(4)
        held = back(y, x, ny)
        ahead = lax.rem(z + x * (1 - jnp.minimum(y, 1)), nz)
        behind = back(z, (1 - x) * (1 - jnp.minimum(y, 1)), nz)

        def rim_send(c, keys):
            device = ((ahead * ny + y) * nx + 1 - x, h)
            src, dst = (kg, hk) if keys else (vg, hv)
            link.copy(src.at[c, held], dst.at[c], rim + 2 * c + 1 - keys, device)

        def rim_wait(c):
            device = ((behind * ny + y) * nx + 1 - x, h)
            link.arrive(hk.at[c], rim + 2 * c, device)
            link.arrive(hv.at[c], rim + 2 * c + 1, device)

        prj = link.take(nh - 1)

        def proj_send():
            for d in range(1, nh):
                hh = hop(h, d, nh)
                link.copy(p_ref.at[:, columns(hh)], pc.at[h], prj + d - 1, (s, hh))

        def proj_wait():
            for d in range(1, nh):
                hh = back(h, d, nh)
                link.arrive(pc.at[hh], prj + d - 1, (s, hh))

        def grads(c):
            cols = pl.ds(pl.multiple_of(y * fs, fs), fs)
            w13 = jnp.concatenate([wb[0, :, cols], wb[1, :, cols]], axis=1)
            w2s = wb[2, :, cols]
            for d in [0] + by_distance(ny):
                if d and c == 0:
                    gather_wait(c, d)
                    if d == 1:
                        rim_send(0, 0)
                        if ny != 4:
                            rim_send(0, 1)
                yy = back(y, d, ny)
                kk, vv = kg[c, yy], vg[c, yy]
                gu = dot(kk, w13)
                g, u = gu[:, :fs], gu[:, fs:]
                dh = dot(vv, w2s)
                sg = jax.nn.sigmoid(g)
                act = g * sg
                dd = jnp.concatenate([dh * u * (sg + act * (1.0 - sg)), dh * act], axis=1).astype(BF16)
                hid = (act * u).astype(BF16)
                t13, t2 = dot_tn(kk, dd), dot_tn(vv, hid)
                if d == 0:
                    acc[:, : 2 * fs] = t13
                    acc[:, 2 * fs:] = t2
                else:
                    acc[:, : 2 * fs] += t13
                    acc[:, 2 * fs:] += t2
            gs[c] = acc[...].astype(BF16).reshape(nz, rp, 3 * fs)

        rsz = [link.take(nz - 1) for c in range(2)]
        exx = [link.take(1) for c in range(2)]
        agz = [link.take(nz - 1) for c in range(2)]
        agy = [link.take((ny - 1) * nz) for c in range(2)]

        def rs_send(c):
            for d in far_first(nz):
                zz = hop(z, d, nz)
                link.copy(gs.at[c, zz], rz.at[c, d - 1], rsz[c] + d - 1, at_z(zz))

        def rs_finish(c):
            total = acc[pl.ds(pl.multiple_of(z * rp, rp), rp), :]
            for d in by_distance(nz):
                link.arrive(rz.at[c, d - 1], rsz[c] + d - 1, at_z(back(z, d, nz)))
                total = total + rz[c, d - 1].astype(F32)
            xs[c] = total.astype(BF16)
            link.copy(xs.at[c], xr.at[c], exx[c], at_x)

        def forward_y(c, zz, d):
            for e in far_first(ny):
                yy = hop(y, e, ny)
                link.copy(ga.at[c, y, zz], ga.at[c, y, zz], agy[c] + (e - 1) * nz + d, at_y(yy))

        def x_finish(c):
            link.arrive(xr.at[c], exx[c], at_x)
            ga[c, y, z] = (xs[c].astype(F32) + xr[c].astype(F32)).astype(BF16)
            for d in far_first(nz):
                link.copy(ga.at[c, y, z], ga.at[c, y, z], agz[c] + d - 1, at_z(hop(z, d, nz)))
            forward_y(c, z, 0)

        def ag_forward(c):
            for d in by_distance(nz):
                zz = back(z, d, nz)
                link.arrive(ga.at[c, y, zz], agz[c] + d - 1, at_z(zz))
                forward_y(c, zz, d)

        def ag_wait(c):
            for e in range(1, ny):
                yy = back(y, e, ny)
                for d in range(nz):
                    zz = back(z, d, nz)
                    link.arrive(ga.at[c, yy, zz], agy[c] + (e - 1) * nz + d, at_y(yy))

        def put(m, value, low):
            xf[m] = value
            hi = value.astype(BF16)
            xh[m] = hi
            if low:
                xl[m] = (value - hi.astype(F32)).astype(BF16)

        def schulz_start(c):
            for m in range(3):
                full = jnp.concatenate(
                    [ga[c, yy].reshape(hd, 3 * fs)[:, m * fs:(m + 1) * fs] for yy in range(ny)], axis=1
                ).astype(F32)
                norm = jnp.sqrt(jnp.sum(full * full, keepdims=True)) + EPSILON
                put(m, full * (1.0 / norm), False)

        def coarse(step, carry):
            grams = [dot_nt(xh[m], xh[m]) for m in range(3)]
            small = [gram.astype(BF16) for gram in grams]
            polys = [(C3 * grams[m] + C5 * dot(small[m], small[m])).astype(BF16) for m in range(3)]
            for m in range(3):
                put(m, C1 * xf[m] + dot(polys[m], xh[m]), True)
            return carry

        def fine(passes):
            grams = [dot_nt(xh[m], xh[m]) for m in range(3)]
            polys = []
            for m in range(3):
                gh = grams[m].astype(BF16)
                gl = (grams[m] - gh.astype(F32)).astype(BF16)
                square = dot(jnp.concatenate([gh, gl, gh][:passes], axis=1),
                             jnp.concatenate([gh, gh, gl][:passes], axis=0))
                polys.append(C3 * grams[m] + C5 * square)
            for m in range(3):
                ph = polys[m].astype(BF16)
                po = (polys[m] - ph.astype(F32)).astype(BF16)
                step_x = dot(jnp.concatenate([ph, po, ph], axis=1),
                             jnp.concatenate([xh[m], xh[m], xl[m]], axis=0))
                put(m, C1 * xf[m] + step_x, True)

        def schulz_coarse():
            lax.fori_loop(0, 2, coarse, 0)

        def schulz_fine(passes):
            for count in passes:
                fine(count)

        def schulz_end(c):
            for m in range(3):
                news[m][...] += LEARN_RATE * xf[m]
                if c == 0:
                    wb[m] = news[m][...].astype(BF16)

        def attend(c):
            qq = qv[c]
            slot = c if c == 0 else 1 - first
            scale = 1.0 / math.sqrt(hd)
            row = lax.broadcasted_iota(jnp.int32, (tok, tok), 0)
            col = lax.broadcasted_iota(jnp.int32, (tok, tok), 1)
            own_ok = col <= row
            rim_ok = col > row + (first * tok if c == 0 else 0)
            own = jnp.where(own_ok, dot_nt(qq, kg[c, y]) * scale, -1e30)
            old = jnp.where(rim_ok, dot_nt(qq, hk[slot]) * scale, -1e30)
            top = jnp.maximum(jnp.max(own, axis=1, keepdims=True), jnp.max(old, axis=1, keepdims=True))
            own = jnp.where(own_ok, jnp.exp(own - top), 0.0)
            old = jnp.where(rim_ok, jnp.exp(old - top), 0.0)
            inv = 1.0 / (jnp.sum(own, axis=1, keepdims=True) + jnp.sum(old, axis=1, keepdims=True))
            return dot((own * inv).astype(BF16), vg[c, y]) + dot((old * inv).astype(BF16), hv[slot])

        def recall(c):
            qq = qv[c]
            g, u = dot(qq, wb[0]), dot(qq, wb[1])
            hid = (g * jax.nn.sigmoid(g) * u).astype(BF16)
            out = dot_nt(hid, wb[2])
            return out * lax.rsqrt(jnp.mean(out * out, axis=1, keepdims=True) + EPSILON)

        mxs = [link.take(nh - 1) for c in range(2)]

        twin = h + 1 - 2 * lax.rem(h, 2)
        near = lax.rem(h + 2, nh)
        far = lax.rem(twin + 2, nh)

        def mix_send(c):
            if nh == 4:
                link.copy(mx.at[c, h], mx.at[c, h], mxs[c], (s, near))
            link.copy(mx.at[c, h], mx.at[c, h], mxs[c] + nh - 2, (s, twin))

        def mix_pass(c):
            if nh == 4:
                link.arrive(mx.at[c, near], mxs[c], (s, near))
                link.copy(mx.at[c, near], mx.at[c, near], mxs[c] + 1, (s, twin))

        def mix_wait(c):
            link.arrive(mx.at[c, twin], mxs[c] + nh - 2, (s, twin))
            if nh == 4:
                link.arrive(mx.at[c, far], mxs[c] + 1, (s, twin))

        def project(c):
            total = dot(mx[c, 0], pc[0])
            for hh in range(1, nh):
                total = total + dot(mx[c, hh], pc[hh])
            st_ref[c] = total.astype(BF16)
            diff = total - tch[c].astype(F32)
            rsd[c] = diff.astype(BF16)
            return jnp.sum((diff * diff).reshape(tok // 8, 8, hd // 128, 128), axis=(0, 2))

        osy = link.take(ny - 1)
        osz = link.take(nz - 1)
        osx = link.take(nx * nh - 1)
        oaz = link.take(nz - 1)
        oay = link.take((ny - 1) * nz)
        lsy, lsz, lsx = link.take(ny - 1), link.take(nz - 1), link.take(nx * nh - 1)
        others = [(dx, dh) for dx in range(nx) for dh in range(nh)][1:]

        def at_xh(dx, dh, sign):
            hh = hop(h, dh, nh) if sign > 0 else back(h, dh, nh)
            xx = hop(x, dx, nx)
            return xx, hh, ((z * ny + y) * nx + xx, hh)

        def stage_grad(unused):
            for hh in range(nh):
                part = (dot_tn(mx[0, hh], rsd[0]) + dot_tn(mx[1, hh], rsd[1])).astype(BF16)
                for yy in range(ny):
                    for zz in range(nz):
                        top = yy * (hd // ny) + (zz // 2) * orow
                        left = (zz % 2) * (hd // 2)
                        ogs[yy, zz, hh] = part[top:top + orow, left:left + hd // 2]
            for d in far_first(ny):
                yy = hop(y, d, ny)
                link.copy(ogs.at[yy], oy.at[d - 1], osy + d - 1, at_y(yy))
                link.copy(ly.at[y], ly.at[y], lsy + d - 1, at_y(yy))

        def stage_y(unused):
            total = ogs[y].astype(F32)
            for d in by_distance(ny):
                yy = back(y, d, ny)
                link.arrive(oy.at[d - 1], osy + d - 1, at_y(yy))
                link.arrive(ly.at[yy], lsy + d - 1, at_y(yy))
                total = total + oy[d - 1].astype(F32)
            ozs[...] = total.astype(BF16)
            lz[z] = jnp.sum(ly[...], axis=0)
            for d in far_first(nz):
                zz = hop(z, d, nz)
                link.copy(ozs.at[zz], oz.at[d - 1], osz + d - 1, at_z(zz))
                link.copy(lz.at[z], lz.at[z], lsz + d - 1, at_z(zz))

        def stage_z(unused):
            total = ozs[z].astype(F32)
            for d in by_distance(nz):
                zz = back(z, d, nz)
                link.arrive(oz.at[d - 1], osz + d - 1, at_z(zz))
                link.arrive(lz.at[zz], lsz + d - 1, at_z(zz))
                total = total + oz[d - 1].astype(F32)
            oxs[...] = total.astype(BF16)
            lx[x, h] = jnp.sum(lz[...], axis=0)
            for i, (dx, dh) in enumerate(others):
                xx, hh, device = at_xh(dx, dh, 1)
                link.copy(oxs.at[hh], ox.at[x, h], osx + i, device)
                link.copy(lx.at[x, h], lx.at[x, h], lsx + i, device)
            ox[x, h] = oxs[h]

        def og_forward(zz, d):
            for e in far_first(ny):
                link.copy(oa.at[y, zz], oa.at[y, zz], oay + (e - 1) * nz + d, at_y(hop(y, e, ny)))

        def stage_x(unused):
            for i, (dx, dh) in enumerate(others):
                xx, hh, device = at_xh(dx, dh, -1)
                link.arrive(ox.at[xx, hh], osx + i, device)
                link.arrive(lx.at[xx, hh], lsx + i, device)
            oa[y, z] = sum(ox[i].astype(F32) for i in range(nx)).astype(BF16)
            for d in far_first(nz):
                link.copy(oa.at[y, z], oa.at[y, z], oaz + d - 1, at_z(hop(z, d, nz)))
            og_forward(z, 0)
            ls_ref[...] = jnp.sum(lx[...], axis=(0, 1))

        def stage_all(part):
            for d in by_distance(nz)[4 * part:4 * part + 4]:
                zz = back(z, d, nz)
                link.arrive(oa.at[y, zz], oaz + d - 1, at_z(zz))
                og_forward(zz, d)

        def stage_wait(unused):
            for e in by_distance(ny):
                yy = back(y, e, ny)
                for d in range(nz):
                    link.arrive(oa.at[yy, back(z, d, nz)], oay + (e - 1) * nz + d, at_y(yy))

        gather_send(0)
        for move in loads[2:]:
            move.wait()
        n2v[...] = w2v[...].T
        for m in range(3):
            wb[m] = news[m][...].astype(BF16)
        for move in loads[:2]:
            move.wait()
        gather_pass()
        if ny == 4:
            rim_send(0, 1)
        gather_send(1)
        proj_send()
        att[0] = recall(0)
        grads(0)
        rs_send(0)
        rim_wait(0)
        mx[0, h] = (att[0] + attend(0)).astype(BF16)
        rs_finish(0)
        x_finish(0)
        mix_send(0)
        for d in by_distance(ny):
            gather_wait(1, d)
        rim_send(1, 1)
        rim_send(1, 0)
        ag_forward(0)
        mix_pass(0)
        rim_wait(1)
        att[1] = attend(1)
        ag_wait(0)
        schulz_start(0)
        schulz_coarse()
        schulz_fine((1, 3, 2))
        schulz_end(0)
        grads(1)
        rs_send(1)
        mx[1, h] = (att[1] + recall(1)).astype(BF16)
        mix_send(1)
        mix_wait(0)
        proj_wait()
        loss = project(0)
        mix_pass(1)
        rs_finish(1)
        mix_wait(1)
        ly[y] = loss + project(1)
        stage_grad(0)
        x_finish(1)
        ag_forward(1)
        stage_y(0)
        stage_z(0)
        stage_x(0)
        ag_wait(1)
        schulz_start(1)
        schulz_coarse()
        stage_all(0)
        schulz_fine((1,))
        stage_all(1)
        schulz_fine((3, 2))
        schulz_end(1)
        n2_ref[...] = n2v[...].T
        stage_wait(0)
        link.drain()

    return body


def make_finish(nz, ny, nh, hd, grad_scale, loss_scale):
    orow = hd // ny // (nz // 2)

    def finish(st, oa, a1, a3, a2, ls, st_ref, og_ref, n1_ref, n3_ref, n2_ref, ls_ref, og, sem):
        moves = [pltpu.make_async_copy(src, dst, sem.at[i]) for i, (src, dst) in enumerate((
            (st, st_ref), (a1, n1_ref), (a3, n3_ref), (a2, n2_ref), (og, og_ref)))]
        for move in moves[:4]:
            move.start()
        for yy in range(ny):
            for zz in range(nz):
                top = yy * (hd // ny) + (zz // 2) * orow
                for hh in range(nh):
                    left = hh * hd + (zz % 2) * (hd // 2)
                    og[top:top + orow, left:left + hd // 2] = oa[yy, zz, hh].astype(F32) * grad_scale
        moves[4].start()
        ls_ref[0, 0] = jnp.sum(ls[...]) * loss_scale
        for move in moves:
            move.wait()

    return finish


def local(nh, query_rows, key_rows, value_rows, first_fast, third_fast, second_fast, out_proj, teacher):
    blocks, tok, hd = query_rows.shape
    ff = first_fast.shape[2]
    nseq = lax.axis_size("seq")
    nx, ny = NX, NY
    if nseq < 16:
        ny = 2
    nz = nseq // (nx * ny)
    width = teacher.shape[2]
    fs, rp = ff // ny, hd // nz
    orow = hd // ny // (nz // 2)
    vm = pltpu.VMEM
    piece = (nh, orow, hd // 2)
    sems = (2 * 2 * (ny - 1) + 4 + (nh - 1) + 2 * (2 * (nz - 1) + 1 + (ny - 1) * nz) + 2 * (nh - 1)
            + 2 * (ny - 1 + nz - 1 + nx * nh - 1) + (nz - 1) + (ny - 1) * nz)
    spec = pl.BlockSpec(memory_space=pltpu.VMEM)
    parts = pl.pallas_call(
        make_body(nz, ny, nx, nh, tok, hd, ff),
        out_shape=(
            pltpu.VMEM((2, tok, hd), BF16),
            pltpu.VMEM((ny, nz) + piece, BF16),
            pltpu.VMEM((hd, ff), F32),
            pltpu.VMEM((hd, ff), F32),
            pltpu.VMEM((ff, hd), F32),
            pltpu.VMEM((8, 128), F32),
        ),
        in_specs=[pl.BlockSpec(memory_space=pl.ANY)] * 8,
        out_specs=(spec,) * 6,
        scratch_shapes=[
            vm((2, tok, hd), BF16), vm((2, tok, hd), BF16),
            vm((2, ny, tok, hd), BF16), vm((2, ny, tok, hd), BF16),
            vm((2, tok, hd), BF16), vm((ff, hd), F32), vm((hd, ff), F32),
            vm((nh, hd, hd), BF16), vm((2, tok, hd), BF16),
            vm((3, hd, ff), BF16), vm((hd, 3 * fs), F32),
            vm((2, nz, rp, 3 * fs), BF16), vm((2, nz - 1, rp, 3 * fs), BF16),
            vm((2, rp, 3 * fs), BF16), vm((2, rp, 3 * fs), BF16),
            vm((2, ny, nz, rp, 3 * fs), BF16),
            vm((3, hd, ff), F32), vm((3, hd, ff), BF16), vm((3, hd, ff), BF16),
            vm((2, tok, hd), F32), vm((2, nh, tok, hd), BF16), vm((2, tok, hd), BF16),
            vm((ny, nz) + piece, BF16), vm((ny - 1, nz) + piece, BF16),
            vm((nz,) + piece, BF16), vm((nz - 1,) + piece, BF16),
            vm(piece, BF16), vm((nx,) + piece, BF16),
            vm((ny, 8, 128), F32), vm((nz, 8, 128), F32), vm((nx, nh, 8, 128), F32),
            pltpu.SemaphoreType.DMA((sems,)), pltpu.SemaphoreType.DMA((sems,)), pltpu.SemaphoreType.DMA((8,)),
        ],
        compiler_params=pltpu.CompilerParams(collective_id=0, has_side_effects=True, vmem_limit_bytes=56 << 20),
        name="student_step",
    )(query_rows, key_rows, value_rows, first_fast[0], third_fast[0], second_fast[0], out_proj, teacher)
    rows = blocks * tok * nseq
    hbm = pl.BlockSpec(memory_space=pl.ANY)
    student, out_grad, n1, n3, n2, loss = pl.pallas_call(
        make_finish(nz, ny, nh, hd, 1.0 / math.sqrt(rows), 1.0 / (rows * width)),
        out_shape=(
            jax.ShapeDtypeStruct((2, tok, hd), BF16),
            jax.ShapeDtypeStruct((hd, width), F32),
            jax.ShapeDtypeStruct((hd, ff), F32),
            jax.ShapeDtypeStruct((hd, ff), F32),
            jax.ShapeDtypeStruct((ff, hd), F32),
            jax.ShapeDtypeStruct((1, 1), F32),
        ),
        in_specs=[spec] * 6,
        out_specs=(hbm,) * 5 + (pl.BlockSpec(memory_space=pltpu.SMEM),),
        scratch_shapes=[vm((hd, width), F32), pltpu.SemaphoreType.DMA((5,))],
        compiler_params=pltpu.CompilerParams(vmem_limit_bytes=8 << 20),
        name="finish",
    )(*parts)
    return (student, out_grad, n1[None], n3[None], n2[None], loss.reshape(()))


def solution(mesh):
    nh = mesh.shape["head"]

    def step(*args):
        return local(nh, *args)

    in_specs = (
        P(None, "seq", "head"),
        P(None, "seq", "head"),
        P(None, "seq", "head"),
        P("head", None, None),
        P("head", None, None),
        P("head", None, None),
        P("head", None),
        P(None, "seq", None),
    )
    out_specs = (
        P(None, "seq", "head"),
        P("head", None),
        P("head", None, None),
        P("head", None, None),
        P("head", None, None),
        P(),
    )
    return jax.shard_map(step, mesh=mesh, in_specs=in_specs, out_specs=out_specs, check_vma=False)
```

```python
import math

import jax
import jax.numpy as jnp
from jax import lax
from jax.experimental import pallas as pl
from jax.experimental.pallas import tpu as pltpu
from jax.sharding import PartitionSpec as P

F32 = jnp.float32
BF16 = jnp.bfloat16
C1, C3, C5 = (3.4445, -4.775, 2.0315)
LEARN_RATE = 0.5
EPSILON = 1e-06
NY, NX = 4, 2


def dot(a, b):
    return lax.dot_general(a, b, (((1,), (0,)), ((), ())), preferred_element_type=F32)


def dot_nt(a, b):
    return lax.dot_general(a, b, (((1,), (1,)), ((), ())), preferred_element_type=F32)


def dot_tn(a, b):
    return lax.dot_general(a, b, (((0,), (0,)), ((), ())), preferred_element_type=F32)


class Link:
    def __init__(self, send, recv):
        self.send, self.recv, self.used, self.open = send, recv, 0, []

    def take(self, count):
        first = self.used
        self.used += count
        return first

    def copy(self, src, dst, index, device):
        made = pltpu.make_async_remote_copy(
            src_ref=src, dst_ref=dst, send_sem=self.send.at[index], recv_sem=self.recv.at[index],
            device_id=device, device_id_type=pl.DeviceIdType.MESH)
        made.start()
        self.open.append(made)

    def arrive(self, dst, index, device):
        pltpu.make_async_remote_copy(
            src_ref=dst, dst_ref=dst, send_sem=self.send.at[index], recv_sem=self.recv.at[index],
            device_id=device, device_id_type=pl.DeviceIdType.MESH).wait_recv()

    def drain(self):
        for made in self.open:
            made.wait_send()


def by_distance(count):
    return sorted(range(1, count), key=lambda d: min(d, count - d))


def far_first(count):
    return by_distance(count)[::-1]


def make_body(nz, ny, nx, nh, tok, hd, ff):
    fs, rp = ff // ny, hd // nz
    orow = hd // ny // (nz // 2)
    nseq = nz * ny * nx

    def body(q_ref, k_ref, v_ref, w1_ref, w3_ref, w2_ref, p_ref, t_ref,
             st_ref, oa, n1_ref, n3_ref, n2_ref, ls_ref,
             hk, hv, kg, vg, qv, w2v, n2v, pc, tch, wb, acc, gs, rz, xs, xr, ga, xf, xh, xl, att, mx, rsd,
             ogs, oy, ozs, oz, oxs, ox, ly, lz, lx, send, recv, tsem):
        s = lax.axis_index("seq")
        h = lax.axis_index("head")
        x = lax.rem(s, nx)
        y = lax.rem(s // nx, ny)
        z = s // (nx * ny)
        news = (n1_ref, n3_ref, n2v)
        link = Link(send, recv)

        def at_z(zz):
            return ((zz * ny + y) * nx + x, h)

        def at_y(yy):
            return ((z * ny + yy) * nx + x, h)

        def hop(i, d, n):
            return lax.rem(i + d, n)

        def back(i, d, n):
            return lax.rem(i + n - d, n)

        at_x = ((z * ny + y) * nx + (1 - x), h)

        def columns(hh):
            return pl.ds(pl.multiple_of(hh * hd, hd), hd)

        loads = []
        for i, (src, dst) in enumerate((
                (k_ref, kg.at[:, y]), (v_ref, vg.at[:, y]), (w1_ref, n1_ref), (w3_ref, n3_ref), (w2_ref, w2v),
                (q_ref, qv), (p_ref.at[:, columns(h)], pc.at[h]), (t_ref.at[:, :, columns(h)], tch))):
            loads.append(pltpu.make_async_copy(src, dst, tsem.at[i]))
            loads[-1].start()
        barrier = pltpu.get_barrier_semaphore()
        partners = [at_z(hop(z, d, nz)) for d in range(1, nz)]
        partners += [at_y(hop(y, d, ny)) for d in range(1, ny)]
        partners += [(s, hop(h, d, nh)) for d in range(1, nh)]
        partners += [((zz * ny + y) * nx + 1 - x, h) for zz in (z, hop(z, 1, nz), back(z, 1, nz))]
        partners += [(at_x[0], hop(h, d, nh)) for d in range(1, nh)]
        for device in partners:
            pl.semaphore_signal(barrier, inc=1, device_id=device, device_id_type=pl.DeviceIdType.MESH)
        pl.semaphore_wait(barrier, len(partners))

        gat = [link.take(2 * (ny - 1)) for c in range(2)]

        def gather_send(c):
            for d in by_distance(ny):
                if c == 0 and d == 2:
                    continue
                device = at_y(hop(y, d, ny))
                pair = ((k_ref, kg, 2), (v_ref, vg, 1))
                for src, dst, i in pair if d == 1 else pair[::-1]:
                    link.copy(src.at[c], dst.at[c, y], gat[c] + 2 * d - i, device)

        def gather_pass():
            if ny == 4:
                for d, ref, i in ((1, kg, 2), (3, vg, 1)):
                    yy = back(y, d, ny)
                    link.arrive(ref.at[0, yy], gat[0] + 2 * d - i, at_y(yy))
                    link.copy(ref.at[0, yy], ref.at[0, yy], gat[0] + 4 - i, at_y(hop(y, d, ny)))

        def gather_wait(c, d):
            yy = back(y, d, ny)
            passed = c == 0 and ny == 4
            if not (passed and d == 1):
                link.arrive(kg.at[c, yy], gat[c] + 2 * d - 2, at_y(yy))
            if not (passed and d == 3):
                link.arrive(vg.at[c, yy], gat[c] + 2 * d - 1, at_y(yy))

        first = 1 - jnp.minimum(s, 1)
        rim = link.take(4)
        held = back(y, x, ny)
        ahead = lax.rem(z + x * (1 - jnp.minimum(y, 1)), nz)
        behind = back(z, (1 - x) * (1 - jnp.minimum(y, 1)), nz)

        def rim_send(c, keys):
            device = ((ahead * ny + y) * nx + 1 - x, h)
            src, dst = (kg, hk) if keys else (vg, hv)
            link.copy(src.at[c, held], dst.at[c], rim + 2 * c + 1 - keys, device)

        def rim_wait(c):
            device = ((behind * ny + y) * nx + 1 - x, h)
            link.arrive(hk.at[c], rim + 2 * c, device)
            link.arrive(hv.at[c], rim + 2 * c + 1, device)

        prj = link.take(nh - 1)

        def proj_send():
            for d in range(1, nh):
                hh = hop(h, d, nh)
                link.copy(p_ref.at[:, columns(hh)], pc.at[h], prj + d - 1, (s, hh))

        def proj_wait():
            for d in range(1, nh):
                hh = back(h, d, nh)
                link.arrive(pc.at[hh], prj + d - 1, (s, hh))

        def grads(c):
            cols = pl.ds(pl.multiple_of(y * fs, fs), fs)
            w13 = jnp.concatenate([wb[0, :, cols], wb[1, :, cols]], axis=1)
            w2s = wb[2, :, cols]
            for d in [0] + by_distance(ny):
                if d and c == 0:
                    gather_wait(c, d)
                    if d == 1:
                        rim_send(0, 0)
                        if ny != 4:
                            rim_send(0, 1)
                yy = back(y, d, ny)
                kk, vv = kg[c, yy], vg[c, yy]
                gu = dot(kk, w13)
                g, u = gu[:, :fs], gu[:, fs:]
                dh = dot(vv, w2s)
                sg = jax.nn.sigmoid(g)
                act = g * sg
                dd = jnp.concatenate([dh * u * (sg + act * (1.0 - sg)), dh * act], axis=1).astype(BF16)
                hid = (act * u).astype(BF16)
                t13, t2 = dot_tn(kk, dd), dot_tn(vv, hid)
                if d == 0:
                    acc[:, : 2 * fs] = t13
                    acc[:, 2 * fs:] = t2
                else:
                    acc[:, : 2 * fs] += t13
                    acc[:, 2 * fs:] += t2
            gs[c] = acc[...].astype(BF16).reshape(nz, rp, 3 * fs)

        rsz = [link.take(nz - 1) for c in range(2)]
        exx = [link.take(1) for c in range(2)]
        agz = [link.take(nz - 1) for c in range(2)]
        agy = [link.take((ny - 1) * nz) for c in range(2)]

        def rs_send(c):
            for d in far_first(nz):
                zz = hop(z, d, nz)
                link.copy(gs.at[c, zz], rz.at[c, d - 1], rsz[c] + d - 1, at_z(zz))

        def rs_finish(c):
            total = acc[pl.ds(pl.multiple_of(z * rp, rp), rp), :]
            for d in by_distance(nz):
                link.arrive(rz.at[c, d - 1], rsz[c] + d - 1, at_z(back(z, d, nz)))
                total = total + rz[c, d - 1].astype(F32)
            xs[c] = total.astype(BF16)
            link.copy(xs.at[c], xr.at[c], exx[c], at_x)

        def forward_y(c, zz, d):
            for e in far_first(ny):
                yy = hop(y, e, ny)
                link.copy(ga.at[c, y, zz], ga.at[c, y, zz], agy[c] + (e - 1) * nz + d, at_y(yy))

        def x_finish(c):
            link.arrive(xr.at[c], exx[c], at_x)
            ga[c, y, z] = (xs[c].astype(F32) + xr[c].astype(F32)).astype(BF16)
            for d in far_first(nz):
                link.copy(ga.at[c, y, z], ga.at[c, y, z], agz[c] + d - 1, at_z(hop(z, d, nz)))
            forward_y(c, z, 0)

        def ag_forward(c):
            for d in by_distance(nz):
                zz = back(z, d, nz)
                link.arrive(ga.at[c, y, zz], agz[c] + d - 1, at_z(zz))
                forward_y(c, zz, d)

        def ag_wait(c):
            for e in range(1, ny):
                yy = back(y, e, ny)
                for d in range(nz):
                    zz = back(z, d, nz)
                    link.arrive(ga.at[c, yy, zz], agy[c] + (e - 1) * nz + d, at_y(yy))

        def put(m, value, low):
            xf[m] = value
            hi = value.astype(BF16)
            xh[m] = hi
            if low:
                xl[m] = (value - hi.astype(F32)).astype(BF16)

        def schulz_start(c):
            row = lax.broadcasted_iota(jnp.int32, (hd, hd), 0)
            col = lax.broadcasted_iota(jnp.int32, (hd, hd), 1)
            for m in range(3):
                for yy in range(ny):
                    xh[m, :, yy * fs:(yy + 1) * fs] = ga[c, yy].reshape(hd, 3 * fs)[:, m * fs:(m + 1) * fs]
            grams, invs = [], []
            for m in range(3):
                gram = dot_nt(xh[m], xh[m])
                square = jnp.sum(jnp.where(row == col, gram, 0.0), keepdims=True)
                invs.append(1.0 / (jnp.sqrt(square) + EPSILON))
                grams.append(gram * (invs[m] * invs[m]))
            polys = []
            for m in range(3):
                small = grams[m].astype(BF16)
                polys.append((C3 * grams[m] + C5 * dot(small, small)).astype(BF16))
            for m in range(3):
                put(m, invs[m] * (C1 * xh[m].astype(F32) + dot(polys[m], xh[m])), False)

        def schulz_coarse():
            grams = [dot_nt(xh[m], xh[m]) for m in range(3)]
            small = [gram.astype(BF16) for gram in grams]
            polys = [(C3 * grams[m] + C5 * dot(small[m], small[m])).astype(BF16) for m in range(3)]
            for m in range(3):
                put(m, C1 * xf[m] + dot(polys[m], xh[m]), True)

        def fine(passes):
            grams = [dot_nt(xh[m], xh[m]) for m in range(3)]
            polys = []
            for m in range(3):
                gh = grams[m].astype(BF16)
                gl = (grams[m] - gh.astype(F32)).astype(BF16)
                square = dot(jnp.concatenate([gh, gl, gh][:passes], axis=1),
                             jnp.concatenate([gh, gh, gl][:passes], axis=0))
                polys.append(C3 * grams[m] + C5 * square)
            for m in range(3):
                ph = polys[m].astype(BF16)
                po = (polys[m] - ph.astype(F32)).astype(BF16)
                step_x = dot(jnp.concatenate([ph, po, ph], axis=1),
                             jnp.concatenate([xh[m], xh[m], xl[m]], axis=0))
                put(m, C1 * xf[m] + step_x, True)

        def schulz_fine(passes):
            for count in passes:
                fine(count)

        def schulz_end(c):
            for m in range(3):
                news[m][...] += LEARN_RATE * xf[m]
                if c == 0:
                    wb[m] = news[m][...].astype(BF16)

        def attend(c):
            qq = qv[c]
            slot = c if c == 0 else 1 - first
            scale = 1.0 / math.sqrt(hd)
            row = lax.broadcasted_iota(jnp.int32, (tok, tok), 0)
            col = lax.broadcasted_iota(jnp.int32, (tok, tok), 1)
            own_ok = col <= row
            rim_ok = col > row + (first * tok if c == 0 else 0)
            own = jnp.where(own_ok, dot_nt(qq, kg[c, y]) * scale, -1e30)
            old = jnp.where(rim_ok, dot_nt(qq, hk[slot]) * scale, -1e30)
            top = jnp.maximum(jnp.max(own, axis=1, keepdims=True), jnp.max(old, axis=1, keepdims=True))
            own = jnp.where(own_ok, jnp.exp(own - top), 0.0)
            old = jnp.where(rim_ok, jnp.exp(old - top), 0.0)
            inv = 1.0 / (jnp.sum(own, axis=1, keepdims=True) + jnp.sum(old, axis=1, keepdims=True))
            return dot((own * inv).astype(BF16), vg[c, y]) + dot((old * inv).astype(BF16), hv[slot])

        def recall(c, top, count):
            qq = qv[c, top:top + count]
            g, u = dot(qq, wb[0]), dot(qq, wb[1])
            hid = (g * jax.nn.sigmoid(g) * u).astype(BF16)
            out = dot_nt(hid, wb[2])
            return out * lax.rsqrt(jnp.mean(out * out, axis=1, keepdims=True) + EPSILON)

        mxs = [link.take(2 * nh - 2) for c in range(2)]

        twin = h + 1 - 2 * lax.rem(h, 2)
        near = lax.rem(h + 2, nh)
        far = lax.rem(twin + 2, nh)

        half = tok // 2

        def rows(c, hh, i):
            return mx.at[c, hh, pl.ds(i * half, half)]

        def mix_send(c, i):
            if nh == 4:
                link.copy(rows(c, h, i), rows(c, h, i), mxs[c] + i, (s, near))
            link.copy(rows(c, h, i), rows(c, h, i), mxs[c] + 2 * nh - 4 + i, (s, twin))

        def mix_pass(c):
            if nh == 4:
                for i in range(2):
                    link.arrive(rows(c, near, i), mxs[c] + i, (s, near))
                    link.copy(rows(c, near, i), rows(c, near, i), mxs[c] + 2 + i, (s, twin))

        def mix_wait(c):
            for i in range(2):
                link.arrive(rows(c, twin, i), mxs[c] + 2 * nh - 4 + i, (s, twin))
                if nh == 4:
                    link.arrive(rows(c, far, i), mxs[c] + 2 + i, (s, twin))

        def project(c):
            total = dot(mx[c, 0], pc[0])
            for hh in range(1, nh):
                total = total + dot(mx[c, hh], pc[hh])
            st_ref[c] = total.astype(BF16)
            diff = total - tch[c].astype(F32)
            rsd[c] = diff.astype(BF16)
            return jnp.sum((diff * diff).reshape(tok // 8, 8, hd // 128, 128), axis=(0, 2))

        osy = link.take(ny - 1)
        osz = link.take(nz - 1)
        osx = link.take(nx * nh - 1)
        oaz = link.take(nz - 1)
        oay = link.take((ny - 1) * nz)
        lsy, lsz, lsx = link.take(ny - 1), link.take(nz - 1), link.take(nx * nh - 1)
        others = [(dx, dh) for dx in range(nx) for dh in range(nh)][1:]

        def at_xh(dx, dh, sign):
            hh = hop(h, dh, nh) if sign > 0 else back(h, dh, nh)
            xx = hop(x, dx, nx)
            return xx, hh, ((z * ny + y) * nx + xx, hh)

        def stage_grad(unused):
            for hh in range(nh):
                part = (dot_tn(mx[0, hh], rsd[0]) + dot_tn(mx[1, hh], rsd[1])).astype(BF16)
                for yy in range(ny):
                    for zz in range(nz):
                        top = yy * (hd // ny) + (zz // 2) * orow
                        left = (zz % 2) * (hd // 2)
                        ogs[yy, zz, hh] = part[top:top + orow, left:left + hd // 2]
            for d in far_first(ny):
                yy = hop(y, d, ny)
                link.copy(ogs.at[yy], oy.at[d - 1], osy + d - 1, at_y(yy))
                link.copy(ly.at[y], ly.at[y], lsy + d - 1, at_y(yy))

        def stage_y(unused):
            total = ogs[y].astype(F32)
            for d in by_distance(ny):
                yy = back(y, d, ny)
                link.arrive(oy.at[d - 1], osy + d - 1, at_y(yy))
                total = total + oy[d - 1].astype(F32)
            ozs[...] = total.astype(BF16)
            for d in far_first(nz):
                zz = hop(z, d, nz)
                link.copy(ozs.at[zz], oz.at[d - 1], osz + d - 1, at_z(zz))

        def stage_z(unused):
            total = ozs[z].astype(F32)
            for d in by_distance(nz):
                zz = back(z, d, nz)
                link.arrive(oz.at[d - 1], osz + d - 1, at_z(zz))
                total = total + oz[d - 1].astype(F32)
            oxs[...] = total.astype(BF16)
            for i, (dx, dh) in enumerate(others):
                xx, hh, device = at_xh(dx, dh, 1)
                link.copy(oxs.at[hh], ox.at[x, h], osx + i, device)
            ox[x, h] = oxs[h]
            for d in by_distance(ny):
                yy = back(y, d, ny)
                link.arrive(ly.at[yy], lsy + d - 1, at_y(yy))
            lz[z] = jnp.sum(ly[...], axis=0)
            for d in far_first(nz):
                link.copy(lz.at[z], lz.at[z], lsz + d - 1, at_z(hop(z, d, nz)))

        def og_forward(zz, d):
            for e in far_first(ny):
                link.copy(oa.at[y, zz], oa.at[y, zz], oay + (e - 1) * nz + d, at_y(hop(y, e, ny)))

        def stage_x(unused):
            for i, (dx, dh) in enumerate(others):
                xx, hh, device = at_xh(dx, dh, -1)
                link.arrive(ox.at[xx, hh], osx + i, device)
            oa[y, z] = sum(ox[i].astype(F32) for i in range(nx)).astype(BF16)
            for d in far_first(nz):
                link.copy(oa.at[y, z], oa.at[y, z], oaz + d - 1, at_z(hop(z, d, nz)))
            og_forward(z, 0)
            for d in by_distance(nz):
                zz = back(z, d, nz)
                link.arrive(lz.at[zz], lsz + d - 1, at_z(zz))
            lx[x, h] = jnp.sum(lz[...], axis=0)
            for i, (dx, dh) in enumerate(others):
                link.copy(lx.at[x, h], lx.at[x, h], lsx + i, at_xh(dx, dh, 1)[2])

        def stage_all(part):
            for d in by_distance(nz)[2 * part:2 * part + (2 if part < 2 else nz)]:
                zz = back(z, d, nz)
                link.arrive(oa.at[y, zz], oaz + d - 1, at_z(zz))
                og_forward(zz, d)

        def stage_wait(unused):
            for i, (dx, dh) in enumerate(others):
                xx, hh, device = at_xh(dx, dh, -1)
                link.arrive(lx.at[xx, hh], lsx + i, device)
            ls_ref[...] = jnp.sum(lx[...], axis=(0, 1))
            for e in by_distance(ny):
                yy = back(y, e, ny)
                for d in range(nz):
                    link.arrive(oa.at[yy, back(z, d, nz)], oay + (e - 1) * nz + d, at_y(yy))

        gather_send(0)
        for move in loads[2:]:
            move.wait()
        n2v[...] = w2v[...].T
        for m in range(3):
            wb[m] = news[m][...].astype(BF16)
        for move in loads[:2]:
            move.wait()
        gather_pass()
        if ny == 4:
            rim_send(0, 1)
        gather_send(1)
        proj_send()
        att[0] = recall(0, 0, tok)
        grads(0)
        rs_send(0)
        rs_finish(0)
        rim_wait(0)
        mx[0, h] = (att[0] + attend(0)).astype(BF16)
        x_finish(0)
        mix_send(0, 0)
        mix_send(0, 1)
        for d in by_distance(ny):
            gather_wait(1, d)
        rim_send(1, 1)
        rim_send(1, 0)
        ag_forward(0)
        mix_pass(0)
        rim_wait(1)
        att[1] = attend(1)
        ag_wait(0)
        schulz_start(0)
        schulz_coarse()
        schulz_fine((1, 3, 2))
        schulz_end(0)
        for i in range(2):
            top = i * half
            mx[1, h, pl.ds(top, half)] = (att[1, top:top + half] + recall(1, top, half)).astype(BF16)
            mix_send(1, i)
        grads(1)
        rs_send(1)
        mix_wait(0)
        proj_wait()
        loss = project(0)
        mix_pass(1)
        rs_finish(1)
        mix_wait(1)
        ly[y] = loss + project(1)
        stage_grad(0)
        x_finish(1)
        stage_y(0)
        ag_forward(1)
        stage_z(0)
        ag_wait(1)
        schulz_start(1)
        schulz_coarse()
        stage_x(0)
        schulz_fine((1,))
        stage_all(0)
        stage_all(1)
        schulz_fine((3,))
        stage_all(2)
        schulz_fine((2,))
        schulz_end(1)
        n2_ref[...] = n2v[...].T
        stage_wait(0)
        link.drain()

    return body


def make_finish(nz, ny, nh, hd, grad_scale, loss_scale):
    orow = hd // ny // (nz // 2)

    def finish(st, oa, a1, a3, a2, ls, st_ref, og_ref, n1_ref, n3_ref, n2_ref, ls_ref, og, sem):
        moves = [pltpu.make_async_copy(src, dst, sem.at[i]) for i, (src, dst) in enumerate((
            (st, st_ref), (a1, n1_ref), (a3, n3_ref), (a2, n2_ref)))]
        for move in moves:
            move.start()
        for yy in range(ny):
            for zz in range(nz):
                top = yy * (hd // ny) + (zz // 2) * orow
                for hh in range(nh):
                    left = hh * hd + (zz % 2) * (hd // 2)
                    og[top:top + orow, left:left + hd // 2] = oa[yy, zz, hh].astype(F32) * grad_scale
            quarter = pl.ds(yy * (hd // ny), hd // ny)
            moves.append(pltpu.make_async_copy(og.at[quarter], og_ref.at[quarter], sem.at[4 + yy]))
            moves[-1].start()
        ls_ref[0, 0] = jnp.sum(ls[...]) * loss_scale
        for move in moves:
            move.wait()

    return finish


def local(nh, query_rows, key_rows, value_rows, first_fast, third_fast, second_fast, out_proj, teacher):
    blocks, tok, hd = query_rows.shape
    ff = first_fast.shape[2]
    nseq = lax.axis_size("seq")
    nx, ny = NX, NY
    if nseq < 16:
        ny = 2
    nz = nseq // (nx * ny)
    width = teacher.shape[2]
    fs, rp = ff // ny, hd // nz
    orow = hd // ny // (nz // 2)
    vm = pltpu.VMEM
    piece = (nh, orow, hd // 2)
    sems = (2 * 2 * (ny - 1) + 4 + (nh - 1) + 2 * (2 * (nz - 1) + 1 + (ny - 1) * nz) + 4 * (nh - 1)
            + 2 * (ny - 1 + nz - 1 + nx * nh - 1) + (nz - 1) + (ny - 1) * nz)
    spec = pl.BlockSpec(memory_space=pltpu.VMEM)
    parts = pl.pallas_call(
        make_body(nz, ny, nx, nh, tok, hd, ff),
        out_shape=(
            pltpu.VMEM((2, tok, hd), BF16),
            pltpu.VMEM((ny, nz) + piece, BF16),
            pltpu.VMEM((hd, ff), F32),
            pltpu.VMEM((hd, ff), F32),
            pltpu.VMEM((ff, hd), F32),
            pltpu.VMEM((8, 128), F32),
        ),
        in_specs=[pl.BlockSpec(memory_space=pl.ANY)] * 8,
        out_specs=(spec,) * 6,
        scratch_shapes=[
            vm((2, tok, hd), BF16), vm((2, tok, hd), BF16),
            vm((2, ny, tok, hd), BF16), vm((2, ny, tok, hd), BF16),
            vm((2, tok, hd), BF16), vm((ff, hd), F32), vm((hd, ff), F32),
            vm((nh, hd, hd), BF16), vm((2, tok, hd), BF16),
            vm((3, hd, ff), BF16), vm((hd, 3 * fs), F32),
            vm((2, nz, rp, 3 * fs), BF16), vm((2, nz - 1, rp, 3 * fs), BF16),
            vm((2, rp, 3 * fs), BF16), vm((2, rp, 3 * fs), BF16),
            vm((2, ny, nz, rp, 3 * fs), BF16),
            vm((3, hd, ff), F32), vm((3, hd, ff), BF16), vm((3, hd, ff), BF16),
            vm((2, tok, hd), F32), vm((2, nh, tok, hd), BF16), vm((2, tok, hd), BF16),
            vm((ny, nz) + piece, BF16), vm((ny - 1, nz) + piece, BF16),
            vm((nz,) + piece, BF16), vm((nz - 1,) + piece, BF16),
            vm(piece, BF16), vm((nx,) + piece, BF16),
            vm((ny, 8, 128), F32), vm((nz, 8, 128), F32), vm((nx, nh, 8, 128), F32),
            pltpu.SemaphoreType.DMA((sems,)), pltpu.SemaphoreType.DMA((sems,)), pltpu.SemaphoreType.DMA((8,)),
        ],
        compiler_params=pltpu.CompilerParams(collective_id=0, has_side_effects=True, vmem_limit_bytes=56 << 20),
        name="student_step",
    )(query_rows, key_rows, value_rows, first_fast[0], third_fast[0], second_fast[0], out_proj, teacher)
    rows = blocks * tok * nseq
    hbm = pl.BlockSpec(memory_space=pl.ANY)
    student, out_grad, n1, n3, n2, loss = pl.pallas_call(
        make_finish(nz, ny, nh, hd, 1.0 / math.sqrt(rows), 1.0 / (rows * width)),
        out_shape=(
            jax.ShapeDtypeStruct((2, tok, hd), BF16),
            jax.ShapeDtypeStruct((hd, width), F32),
            jax.ShapeDtypeStruct((hd, ff), F32),
            jax.ShapeDtypeStruct((hd, ff), F32),
            jax.ShapeDtypeStruct((ff, hd), F32),
            jax.ShapeDtypeStruct((1, 1), F32),
        ),
        in_specs=[spec] * 6,
        out_specs=(hbm,) * 5 + (pl.BlockSpec(memory_space=pltpu.SMEM),),
        scratch_shapes=[vm((hd, width), F32), pltpu.SemaphoreType.DMA((4 + ny,))],
        compiler_params=pltpu.CompilerParams(vmem_limit_bytes=8 << 20),
        name="finish",
    )(*parts)
    return (student, out_grad, n1[None], n3[None], n2[None], loss.reshape(()))


def solution(mesh):
    nh = mesh.shape["head"]

    def step(*args):
        return local(nh, *args)

    in_specs = (
        P(None, "seq", "head"),
        P(None, "seq", "head"),
        P(None, "seq", "head"),
        P("head", None, None),
        P("head", None, None),
        P("head", None, None),
        P("head", None),
        P(None, "seq", None),
    )
    out_specs = (
        P(None, "seq", "head"),
        P("head", None),
        P("head", None, None),
        P("head", None, None),
        P("head", None, None),
        P(),
    )
    return jax.shard_map(step, mesh=mesh, in_specs=in_specs, out_specs=out_specs, check_vma=False)
```

```python
import math

import jax
import jax.numpy as jnp
from jax import lax
from jax.experimental import pallas as pl
from jax.experimental.pallas import tpu as pltpu
from jax.sharding import PartitionSpec as P

F32 = jnp.float32
BF16 = jnp.bfloat16
C1, C3, C5 = (3.4445, -4.775, 2.0315)
LEARN_RATE = 0.5
EPSILON = 1e-06
NY, NX = 4, 2


def dot(a, b):
    return lax.dot_general(a, b, (((1,), (0,)), ((), ())), preferred_element_type=F32)


def dot_nt(a, b):
    return lax.dot_general(a, b, (((1,), (1,)), ((), ())), preferred_element_type=F32)


def dot_tn(a, b):
    return lax.dot_general(a, b, (((0,), (0,)), ((), ())), preferred_element_type=F32)


class Link:
    def __init__(self, send, recv):
        self.send, self.recv, self.used, self.open = send, recv, 0, []

    def take(self, count):
        first = self.used
        self.used += count
        return first

    def copy(self, src, dst, index, device):
        made = pltpu.make_async_remote_copy(
            src_ref=src, dst_ref=dst, send_sem=self.send.at[index], recv_sem=self.recv.at[index],
            device_id=device, device_id_type=pl.DeviceIdType.MESH)
        made.start()
        self.open.append(made)

    def arrive(self, dst, index, device):
        pltpu.make_async_remote_copy(
            src_ref=dst, dst_ref=dst, send_sem=self.send.at[index], recv_sem=self.recv.at[index],
            device_id=device, device_id_type=pl.DeviceIdType.MESH).wait_recv()

    def drain(self):
        for made in self.open:
            made.wait_send()


def by_distance(count):
    return sorted(range(1, count), key=lambda d: min(d, count - d))


def far_first(count):
    return by_distance(count)[::-1]


def make_body(nz, ny, nx, nh, tok, hd, ff):
    fs, rp = ff // ny, hd // nz
    orow = hd // ny // (nz // 2)
    nseq = nz * ny * nx

    def body(q_ref, k_ref, v_ref, w1_ref, w3_ref, w2_ref, p_ref, t_ref,
             st_ref, oa, n1_ref, n3_ref, n2_ref, ls_ref,
             hk, hv, kg, vg, qv, w2v, n2v, pc, tch, wb, acc, gs, rz, xs, xr, ga, xf, xh, xl, att, mx, rsd,
             ogs, oy, ozs, oz, oxs, ox, ly, lz, lx, send, recv, tsem):
        s = lax.axis_index("seq")
        h = lax.axis_index("head")
        x = lax.rem(s, nx)
        y = lax.rem(s // nx, ny)
        z = s // (nx * ny)
        news = (n1_ref, n3_ref, n2v)
        link = Link(send, recv)

        def at_z(zz):
            return ((zz * ny + y) * nx + x, h)

        def at_y(yy):
            return ((z * ny + yy) * nx + x, h)

        def hop(i, d, n):
            return lax.rem(i + d, n)

        def back(i, d, n):
            return lax.rem(i + n - d, n)

        at_x = ((z * ny + y) * nx + (1 - x), h)

        def columns(hh):
            return pl.ds(pl.multiple_of(hh * hd, hd), hd)

        loads = []
        for i, (src, dst) in enumerate((
                (k_ref, kg.at[:, y]), (v_ref, vg.at[:, y]), (w1_ref, n1_ref), (w3_ref, n3_ref), (w2_ref, w2v),
                (q_ref, qv), (p_ref.at[:, columns(h)], pc.at[h]), (t_ref.at[:, :, columns(h)], tch))):
            loads.append(pltpu.make_async_copy(src, dst, tsem.at[i]))
            loads[-1].start()
        barrier = pltpu.get_barrier_semaphore()
        partners = [at_z(hop(z, d, nz)) for d in range(1, nz)]
        partners += [at_y(hop(y, d, ny)) for d in range(1, ny)]
        partners += [(s, hop(h, d, nh)) for d in range(1, nh)]
        partners += [((zz * ny + y) * nx + 1 - x, h) for zz in (z, hop(z, 1, nz), back(z, 1, nz))]
        partners += [(at_x[0], hop(h, d, nh)) for d in range(1, nh)]
        for device in partners:
            pl.semaphore_signal(barrier, inc=1, device_id=device, device_id_type=pl.DeviceIdType.MESH)
        pl.semaphore_wait(barrier, len(partners))

        gat = [link.take(2 * (ny - 1)) for c in range(2)]

        def gather_send(c):
            for d in by_distance(ny):
                if c == 0 and d == 2:
                    continue
                device = at_y(hop(y, d, ny))
                pair = ((k_ref, kg, 2), (v_ref, vg, 1))
                for src, dst, i in pair if d == 1 else pair[::-1]:
                    link.copy(src.at[c], dst.at[c, y], gat[c] + 2 * d - i, device)

        def gather_pass():
            if ny == 4:
                for d, ref, i in ((1, kg, 2), (3, vg, 1)):
                    yy = back(y, d, ny)
                    link.arrive(ref.at[0, yy], gat[0] + 2 * d - i, at_y(yy))
                    link.copy(ref.at[0, yy], ref.at[0, yy], gat[0] + 4 - i, at_y(hop(y, d, ny)))

        def gather_wait(c, d):
            yy = back(y, d, ny)
            passed = c == 0 and ny == 4
            if not (passed and d == 1):
                link.arrive(kg.at[c, yy], gat[c] + 2 * d - 2, at_y(yy))
            if not (passed and d == 3):
                link.arrive(vg.at[c, yy], gat[c] + 2 * d - 1, at_y(yy))

        first = 1 - jnp.minimum(s, 1)
        rim = link.take(4)
        held = back(y, x, ny)
        ahead = lax.rem(z + x * (1 - jnp.minimum(y, 1)), nz)
        behind = back(z, (1 - x) * (1 - jnp.minimum(y, 1)), nz)

        def rim_send(c, keys):
            device = ((ahead * ny + y) * nx + 1 - x, h)
            src, dst = (kg, hk) if keys else (vg, hv)
            link.copy(src.at[c, held], dst.at[c], rim + 2 * c + 1 - keys, device)

        def rim_wait(c):
            device = ((behind * ny + y) * nx + 1 - x, h)
            link.arrive(hk.at[c], rim + 2 * c, device)
            link.arrive(hv.at[c], rim + 2 * c + 1, device)

        prj = link.take(nh - 1)

        def proj_send():
            for d in range(1, nh):
                hh = hop(h, d, nh)
                link.copy(p_ref.at[:, columns(hh)], pc.at[h], prj + d - 1, (s, hh))

        def proj_wait():
            for d in range(1, nh):
                hh = back(h, d, nh)
                link.arrive(pc.at[hh], prj + d - 1, (s, hh))

        def grads(c):
            cols = pl.ds(pl.multiple_of(y * fs, fs), fs)
            w13 = jnp.concatenate([wb[0, :, cols], wb[1, :, cols]], axis=1)
            w2s = wb[2, :, cols]
            for d in [0] + by_distance(ny):
                if d and c == 0:
                    gather_wait(c, d)
                    if d == 1:
                        rim_send(0, 0)
                        if ny != 4:
                            rim_send(0, 1)
                yy = back(y, d, ny)
                kk, vv = kg[c, yy], vg[c, yy]
                gu = dot(kk, w13)
                g, u = gu[:, :fs], gu[:, fs:]
                dh = dot(vv, w2s)
                sg = jax.nn.sigmoid(g)
                act = g * sg
                dd = jnp.concatenate([dh * u * (sg + act * (1.0 - sg)), dh * act], axis=1).astype(BF16)
                hid = (act * u).astype(BF16)
                t13, t2 = dot_tn(kk, dd), dot_tn(vv, hid)
                if d == 0:
                    acc[:, : 2 * fs] = t13
                    acc[:, 2 * fs:] = t2
                else:
                    acc[:, : 2 * fs] += t13
                    acc[:, 2 * fs:] += t2
            gs[c] = acc[...].astype(BF16).reshape(nz, rp, 3 * fs)

        rsz = [link.take(nz - 1) for c in range(2)]
        exx = [link.take(1) for c in range(2)]
        agz = [link.take(nz - 1) for c in range(2)]
        agy = [link.take((ny - 1) * nz) for c in range(2)]

        def rs_send(c):
            for d in far_first(nz):
                zz = hop(z, d, nz)
                link.copy(gs.at[c, zz], rz.at[c, d - 1], rsz[c] + d - 1, at_z(zz))

        def rs_finish(c):
            total = acc[pl.ds(pl.multiple_of(z * rp, rp), rp), :]
            for d in by_distance(nz):
                link.arrive(rz.at[c, d - 1], rsz[c] + d - 1, at_z(back(z, d, nz)))
                total = total + rz[c, d - 1].astype(F32)
            xs[c] = total.astype(BF16)
            link.copy(xs.at[c], xr.at[c], exx[c], at_x)

        def forward_y(c, zz, d):
            for e in far_first(ny):
                yy = hop(y, e, ny)
                link.copy(ga.at[c, y, zz], ga.at[c, y, zz], agy[c] + (e - 1) * nz + d, at_y(yy))

        def x_finish(c):
            link.arrive(xr.at[c], exx[c], at_x)
            ga[c, y, z] = (xs[c].astype(F32) + xr[c].astype(F32)).astype(BF16)
            for d in far_first(nz):
                link.copy(ga.at[c, y, z], ga.at[c, y, z], agz[c] + d - 1, at_z(hop(z, d, nz)))
            forward_y(c, z, 0)

        def ag_forward(c):
            for d in by_distance(nz):
                zz = back(z, d, nz)
                link.arrive(ga.at[c, y, zz], agz[c] + d - 1, at_z(zz))
                forward_y(c, zz, d)

        def ag_wait(c):
            for e in range(1, ny):
                yy = back(y, e, ny)
                for d in range(nz):
                    zz = back(z, d, nz)
                    link.arrive(ga.at[c, yy, zz], agy[c] + (e - 1) * nz + d, at_y(yy))

        def put(m, value, low):
            xf[m] = value
            hi = value.astype(BF16)
            xh[m] = hi
            if low:
                xl[m] = (value - hi.astype(F32)).astype(BF16)

        def schulz_start(c):
            row = lax.broadcasted_iota(jnp.int32, (hd, hd), 0)
            col = lax.broadcasted_iota(jnp.int32, (hd, hd), 1)
            for m in range(3):
                for yy in range(ny):
                    xh[m, :, yy * fs:(yy + 1) * fs] = ga[c, yy].reshape(hd, 3 * fs)[:, m * fs:(m + 1) * fs]
            grams, invs = [], []
            for m in range(3):
                gram = dot_nt(xh[m], xh[m])
                square = jnp.sum(jnp.where(row == col, gram, 0.0), keepdims=True)
                invs.append(1.0 / (jnp.sqrt(square) + EPSILON))
                grams.append(gram * (invs[m] * invs[m]))
            polys = []
            for m in range(3):
                small = grams[m].astype(BF16)
                polys.append((C3 * grams[m] + C5 * dot(small, small)).astype(BF16))
            for m in range(3):
                put(m, invs[m] * (C1 * xh[m].astype(F32) + dot(polys[m], xh[m])), False)

        def schulz_coarse():
            grams = [dot_nt(xh[m], xh[m]) for m in range(3)]
            small = [gram.astype(BF16) for gram in grams]
            polys = [(C3 * grams[m] + C5 * dot(small[m], small[m])).astype(BF16) for m in range(3)]
            for m in range(3):
                put(m, C1 * xf[m] + dot(polys[m], xh[m]), True)

        def fine(passes):
            grams = [dot_nt(xh[m], xh[m]) for m in range(3)]
            polys = []
            for m in range(3):
                gh = grams[m].astype(BF16)
                gl = (grams[m] - gh.astype(F32)).astype(BF16)
                square = dot(jnp.concatenate([gh, gl, gh][:passes], axis=1),
                             jnp.concatenate([gh, gh, gl][:passes], axis=0))
                polys.append(C3 * grams[m] + C5 * square)
            for m in range(3):
                ph = polys[m].astype(BF16)
                po = (polys[m] - ph.astype(F32)).astype(BF16)
                step_x = dot(jnp.concatenate([ph, po, ph], axis=1),
                             jnp.concatenate([xh[m], xh[m], xl[m]], axis=0))
                put(m, C1 * xf[m] + step_x, True)

        def schulz_fine(passes):
            for count in passes:
                fine(count)

        def schulz_end(c):
            for m in range(3):
                news[m][...] += LEARN_RATE * xf[m]
                if c == 0:
                    wb[m] = news[m][...].astype(BF16)

        def attend(c):
            qq = qv[c]
            slot = c if c == 0 else 1 - first
            scale = 1.0 / math.sqrt(hd)
            row = lax.broadcasted_iota(jnp.int32, (tok, tok), 0)
            col = lax.broadcasted_iota(jnp.int32, (tok, tok), 1)
            own_ok = col <= row
            rim_ok = col > row + (first * tok if c == 0 else 0)
            own = jnp.where(own_ok, dot_nt(qq, kg[c, y]) * scale, -1e30)
            old = jnp.where(rim_ok, dot_nt(qq, hk[slot]) * scale, -1e30)
            top = jnp.maximum(jnp.max(own, axis=1, keepdims=True), jnp.max(old, axis=1, keepdims=True))
            own = jnp.where(own_ok, jnp.exp(own - top), 0.0)
            old = jnp.where(rim_ok, jnp.exp(old - top), 0.0)
            inv = 1.0 / (jnp.sum(own, axis=1, keepdims=True) + jnp.sum(old, axis=1, keepdims=True))
            return dot((own * inv).astype(BF16), vg[c, y]) + dot((old * inv).astype(BF16), hv[slot])

        def recall(c, top, count):
            qq = qv[c, top:top + count]
            g, u = dot(qq, wb[0]), dot(qq, wb[1])
            hid = (g * jax.nn.sigmoid(g) * u).astype(BF16)
            out = dot_nt(hid, wb[2])
            return out * lax.rsqrt(jnp.mean(out * out, axis=1, keepdims=True) + EPSILON)

        mxs = [link.take(2 * nh - 2) for c in range(2)]

        twin = h + 1 - 2 * lax.rem(h, 2)
        near = lax.rem(h + 2, nh)
        far = lax.rem(twin + 2, nh)

        half = tok // 2

        def rows(c, hh, i):
            return mx.at[c, hh, pl.ds(i * half, half)]

        def mix_send(c, i):
            if nh == 4:
                link.copy(rows(c, h, i), rows(c, h, i), mxs[c] + i, (s, near))
            link.copy(rows(c, h, i), rows(c, h, i), mxs[c] + 2 * nh - 4 + i, (s, twin))

        def mix_pass(c):
            if nh == 4:
                for i in range(2):
                    link.arrive(rows(c, near, i), mxs[c] + i, (s, near))
                    link.copy(rows(c, near, i), rows(c, near, i), mxs[c] + 2 + i, (s, twin))

        def mix_wait(c):
            for i in range(2):
                link.arrive(rows(c, twin, i), mxs[c] + 2 * nh - 4 + i, (s, twin))
                if nh == 4:
                    link.arrive(rows(c, far, i), mxs[c] + 2 + i, (s, twin))

        def project(c):
            total = dot(mx[c, 0], pc[0])
            for hh in range(1, nh):
                total = total + dot(mx[c, hh], pc[hh])
            st_ref[c] = total.astype(BF16)
            diff = total - tch[c].astype(F32)
            rsd[c] = diff.astype(BF16)
            return jnp.sum((diff * diff).reshape(tok // 8, 8, hd // 128, 128), axis=(0, 2))

        osy = link.take(ny - 1)
        osz = link.take(nz - 1)
        osx = link.take(nx * nh - 1)
        oaz = link.take(nz - 1)
        oay = link.take((ny - 1) * nz)
        lsy, lsz, lsx = link.take(ny - 1), link.take(nz - 1), link.take(nx * nh - 1)
        others = [(dx, dh) for dx in range(nx) for dh in range(nh)][1:]

        def at_xh(dx, dh, sign):
            hh = hop(h, dh, nh) if sign > 0 else back(h, dh, nh)
            xx = hop(x, dx, nx)
            return xx, hh, ((z * ny + y) * nx + xx, hh)

        def stage_grad(unused):
            for hh in range(nh):
                part = (dot_tn(mx[0, hh], rsd[0]) + dot_tn(mx[1, hh], rsd[1])).astype(BF16)
                for yy in range(ny):
                    for zz in range(nz):
                        top = yy * (hd // ny) + (zz // 2) * orow
                        left = (zz % 2) * (hd // 2)
                        ogs[yy, zz, hh] = part[top:top + orow, left:left + hd // 2]
            for d in far_first(ny):
                yy = hop(y, d, ny)
                link.copy(ogs.at[yy], oy.at[d - 1], osy + d - 1, at_y(yy))
                link.copy(ly.at[y], ly.at[y], lsy + d - 1, at_y(yy))

        def stage_y(unused):
            total = ogs[y].astype(F32)
            for d in by_distance(ny):
                yy = back(y, d, ny)
                link.arrive(oy.at[d - 1], osy + d - 1, at_y(yy))
                total = total + oy[d - 1].astype(F32)
            ozs[...] = total.astype(BF16)
            for d in far_first(nz):
                zz = hop(z, d, nz)
                link.copy(ozs.at[zz], oz.at[d - 1], osz + d - 1, at_z(zz))

        def stage_z(unused):
            total = ozs[z].astype(F32)
            for d in by_distance(nz):
                zz = back(z, d, nz)
                link.arrive(oz.at[d - 1], osz + d - 1, at_z(zz))
                total = total + oz[d - 1].astype(F32)
            oxs[...] = total.astype(BF16)
            for i, (dx, dh) in enumerate(others):
                xx, hh, device = at_xh(dx, dh, 1)
                link.copy(oxs.at[hh], ox.at[x, h], osx + i, device)
            ox[x, h] = oxs[h]
            for d in by_distance(ny):
                yy = back(y, d, ny)
                link.arrive(ly.at[yy], lsy + d - 1, at_y(yy))
            lz[z] = jnp.sum(ly[...], axis=0)
            for d in far_first(nz):
                link.copy(lz.at[z], lz.at[z], lsz + d - 1, at_z(hop(z, d, nz)))

        def og_forward(zz, d):
            for e in far_first(ny):
                link.copy(oa.at[y, zz], oa.at[y, zz], oay + (e - 1) * nz + d, at_y(hop(y, e, ny)))

        def stage_x(unused):
            for i, (dx, dh) in enumerate(others):
                xx, hh, device = at_xh(dx, dh, -1)
                link.arrive(ox.at[xx, hh], osx + i, device)
            oa[y, z] = sum(ox[i].astype(F32) for i in range(nx)).astype(BF16)
            for d in far_first(nz):
                link.copy(oa.at[y, z], oa.at[y, z], oaz + d - 1, at_z(hop(z, d, nz)))
            og_forward(z, 0)
            for d in by_distance(nz):
                zz = back(z, d, nz)
                link.arrive(lz.at[zz], lsz + d - 1, at_z(zz))
            lx[x, h] = jnp.sum(lz[...], axis=0)
            for i, (dx, dh) in enumerate(others):
                link.copy(lx.at[x, h], lx.at[x, h], lsx + i, at_xh(dx, dh, 1)[2])

        def stage_all(part):
            for d in by_distance(nz)[2 * part:2 * part + (2 if part < 2 else nz)]:
                zz = back(z, d, nz)
                link.arrive(oa.at[y, zz], oaz + d - 1, at_z(zz))
                og_forward(zz, d)

        def stage_wait(unused):
            for i, (dx, dh) in enumerate(others):
                xx, hh, device = at_xh(dx, dh, -1)
                link.arrive(lx.at[xx, hh], lsx + i, device)
            ls_ref[...] = jnp.sum(lx[...], axis=(0, 1))
            for e in by_distance(ny):
                yy = back(y, e, ny)
                for d in range(nz):
                    link.arrive(oa.at[yy, back(z, d, nz)], oay + (e - 1) * nz + d, at_y(yy))

        gather_send(0)
        for move in loads[2:]:
            move.wait()
        n2v[...] = w2v[...].T
        for m in range(3):
            wb[m] = news[m][...].astype(BF16)
        for move in loads[:2]:
            move.wait()
        gather_pass()
        if ny == 4:
            rim_send(0, 1)
        gather_send(1)
        proj_send()
        att[0] = recall(0, 0, tok)
        grads(0)
        rs_send(0)
        rs_finish(0)
        rim_wait(0)
        mx[0, h] = (att[0] + attend(0)).astype(BF16)
        x_finish(0)
        mix_send(0, 0)
        mix_send(0, 1)
        gather_wait(1, 1)
        rim_send(1, 1)
        rim_send(1, 0)
        ag_forward(0)
        for d in range(2, ny):
            gather_wait(1, d)
        mix_pass(0)
        rim_wait(1)
        att[1] = attend(1)
        ag_wait(0)
        schulz_start(0)
        schulz_coarse()
        schulz_fine((1, 3, 2))
        schulz_end(0)
        for i in range(2):
            top = i * half
            mx[1, h, pl.ds(top, half)] = (att[1, top:top + half] + recall(1, top, half)).astype(BF16)
            mix_send(1, i)
        grads(1)
        rs_send(1)
        mix_wait(0)
        proj_wait()
        loss = project(0)
        mix_pass(1)
        rs_finish(1)
        mix_wait(1)
        ly[y] = loss + project(1)
        stage_grad(0)
        x_finish(1)
        stage_y(0)
        ag_forward(1)
        stage_z(0)
        ag_wait(1)
        schulz_start(1)
        schulz_coarse()
        stage_x(0)
        schulz_fine((1,))
        stage_all(0)
        stage_all(1)
        schulz_fine((3,))
        stage_all(2)
        schulz_fine((2,))
        schulz_end(1)
        n2_ref[...] = n2v[...].T
        stage_wait(0)
        link.drain()

    return body


def make_finish(nz, ny, nh, hd, grad_scale, loss_scale):
    orow = hd // ny // (nz // 2)

    def finish(st, oa, a1, a3, a2, ls, st_ref, og_ref, n1_ref, n3_ref, n2_ref, ls_ref, og, sem):
        moves = [pltpu.make_async_copy(src, dst, sem.at[i]) for i, (src, dst) in enumerate((
            (st, st_ref), (a1, n1_ref), (a3, n3_ref), (a2, n2_ref)))]
        for move in moves:
            move.start()
        for yy in range(ny):
            for zz in range(nz):
                top = yy * (hd // ny) + (zz // 2) * orow
                for hh in range(nh):
                    left = hh * hd + (zz % 2) * (hd // 2)
                    og[top:top + orow, left:left + hd // 2] = oa[yy, zz, hh].astype(F32) * grad_scale
            quarter = pl.ds(yy * (hd // ny), hd // ny)
            moves.append(pltpu.make_async_copy(og.at[quarter], og_ref.at[quarter], sem.at[4 + yy]))
            moves[-1].start()
        ls_ref[0, 0] = jnp.sum(ls[...]) * loss_scale
        for move in moves:
            move.wait()

    return finish


def local(nh, query_rows, key_rows, value_rows, first_fast, third_fast, second_fast, out_proj, teacher):
    blocks, tok, hd = query_rows.shape
    ff = first_fast.shape[2]
    nseq = lax.axis_size("seq")
    nx, ny = NX, NY
    if nseq < 16:
        ny = 2
    nz = nseq // (nx * ny)
    width = teacher.shape[2]
    fs, rp = ff // ny, hd // nz
    orow = hd // ny // (nz // 2)
    vm = pltpu.VMEM
    piece = (nh, orow, hd // 2)
    sems = (2 * 2 * (ny - 1) + 4 + (nh - 1) + 2 * (2 * (nz - 1) + 1 + (ny - 1) * nz) + 4 * (nh - 1)
            + 2 * (ny - 1 + nz - 1 + nx * nh - 1) + (nz - 1) + (ny - 1) * nz)
    spec = pl.BlockSpec(memory_space=pltpu.VMEM)
    parts = pl.pallas_call(
        make_body(nz, ny, nx, nh, tok, hd, ff),
        out_shape=(
            pltpu.VMEM((2, tok, hd), BF16),
            pltpu.VMEM((ny, nz) + piece, BF16),
            pltpu.VMEM((hd, ff), F32),
            pltpu.VMEM((hd, ff), F32),
            pltpu.VMEM((ff, hd), F32),
            pltpu.VMEM((8, 128), F32),
        ),
        in_specs=[pl.BlockSpec(memory_space=pl.ANY)] * 8,
        out_specs=(spec,) * 6,
        scratch_shapes=[
            vm((2, tok, hd), BF16), vm((2, tok, hd), BF16),
            vm((2, ny, tok, hd), BF16), vm((2, ny, tok, hd), BF16),
            vm((2, tok, hd), BF16), vm((ff, hd), F32), vm((hd, ff), F32),
            vm((nh, hd, hd), BF16), vm((2, tok, hd), BF16),
            vm((3, hd, ff), BF16), vm((hd, 3 * fs), F32),
            vm((2, nz, rp, 3 * fs), BF16), vm((2, nz - 1, rp, 3 * fs), BF16),
            vm((2, rp, 3 * fs), BF16), vm((2, rp, 3 * fs), BF16),
            vm((2, ny, nz, rp, 3 * fs), BF16),
            vm((3, hd, ff), F32), vm((3, hd, ff), BF16), vm((3, hd, ff), BF16),
            vm((2, tok, hd), F32), vm((2, nh, tok, hd), BF16), vm((2, tok, hd), BF16),
            vm((ny, nz) + piece, BF16), vm((ny - 1, nz) + piece, BF16),
            vm((nz,) + piece, BF16), vm((nz - 1,) + piece, BF16),
            vm(piece, BF16), vm((nx,) + piece, BF16),
            vm((ny, 8, 128), F32), vm((nz, 8, 128), F32), vm((nx, nh, 8, 128), F32),
            pltpu.SemaphoreType.DMA((sems,)), pltpu.SemaphoreType.DMA((sems,)), pltpu.SemaphoreType.DMA((8,)),
        ],
        compiler_params=pltpu.CompilerParams(collective_id=0, has_side_effects=True, vmem_limit_bytes=56 << 20),
        name="student_step",
    )(query_rows, key_rows, value_rows, first_fast[0], third_fast[0], second_fast[0], out_proj, teacher)
    rows = blocks * tok * nseq
    hbm = pl.BlockSpec(memory_space=pl.ANY)
    student, out_grad, n1, n3, n2, loss = pl.pallas_call(
        make_finish(nz, ny, nh, hd, 1.0 / math.sqrt(rows), 1.0 / (rows * width)),
        out_shape=(
            jax.ShapeDtypeStruct((2, tok, hd), BF16),
            jax.ShapeDtypeStruct((hd, width), F32),
            jax.ShapeDtypeStruct((hd, ff), F32),
            jax.ShapeDtypeStruct((hd, ff), F32),
            jax.ShapeDtypeStruct((ff, hd), F32),
            jax.ShapeDtypeStruct((1, 1), F32),
        ),
        in_specs=[spec] * 6,
        out_specs=(hbm,) * 5 + (pl.BlockSpec(memory_space=pltpu.SMEM),),
        scratch_shapes=[vm((hd, width), F32), pltpu.SemaphoreType.DMA((4 + ny,))],
        compiler_params=pltpu.CompilerParams(vmem_limit_bytes=8 << 20),
        name="finish",
    )(*parts)
    return (student, out_grad, n1[None], n3[None], n2[None], loss.reshape(()))


def solution(mesh):
    nh = mesh.shape["head"]

    def step(*args):
        return local(nh, *args)

    in_specs = (
        P(None, "seq", "head"),
        P(None, "seq", "head"),
        P(None, "seq", "head"),
        P("head", None, None),
        P("head", None, None),
        P("head", None, None),
        P("head", None),
        P(None, "seq", None),
    )
    out_specs = (
        P(None, "seq", "head"),
        P("head", None),
        P("head", None, None),
        P("head", None, None),
        P("head", None, None),
        P(),
    )
    return jax.shard_map(step, mesh=mesh, in_specs=in_specs, out_specs=out_specs, check_vma=False)
```
